32 devices in a mesh: ctx: 8 (over y, x, core), exp: 4 (over z).
Axes of the slice: x: 2, y: 2, z: 4, core: 2. Of those that a mesh axis runs over, the one named last changes fastest.
Arguments:
- mixer_input: bfloat16 [8192, 4096], P('ctx', 'exp'), may hold values from -6 to 6
- scale_exponent: int32 [64, 64], P('ctx', 'exp'), may hold values from -1 to 1
- step_size: float32 [64, 8192], P('exp', 'ctx'), may hold values from 0.25 to 1
- decay_log: float32 [64, 8192], P('exp', 'ctx'), may hold values from -1.2 to 0
- state_input: bfloat16 [8192, 128], P('ctx'), may hold values from -6 to 6
- state_output: bfloat16 [8192, 128], P('ctx'), may hold values from -0.5 to 0.5
- skip_gain: float32 [64], P('exp'), may hold values from 0.5 to 1.5
- gate_input: bfloat16 [8192, 4096], P('ctx', 'exp'), may hold values from -6 to 6
- norm_gain: float32 [4096], P('exp'), may hold values from 0.25 to 1.75
- up_weight: bfloat16 [4096, 3072], P('ctx', 'exp'), may hold values from -0.09375 to 0.09375
- down_weight: bfloat16 [3072, 4096], P('exp', 'ctx'), may hold values from -0.15625 to 0.15625
- expert_slot: int32 [8192], P('ctx'), may hold values from 0 to 256, as said below
- gate_prob: float32 [8192], P('ctx'), may hold values from 0.2 to 1
Outputs:
- layer_out: bfloat16 [8192, 4096], P('ctx', 'exp')
The draws below stay inside these ranges and needn't reach their ends.
Inputs may be any that keep to these rules, and one draw needn't show every extreme that they name: `expert_slot`: within each aligned block of 1024 tokens, the tokens routed to the expert carry the distinct slots 0 to k - 1 for some k of at most 256, and all other tokens carry 256; in some block k equals 256.
All inputs are finite; a program needn't handle non-finite values.
Results may differ from the reference program's by a relative error of at most 0.0085.
Values may be sent and summed in bfloat16 or wider, within the bound.
No kernel may reach another device: no remote copies, remote signals or barrier semaphores. Data moves between devices by JAX's collectives and lax.ppermute only.
A program may use at most 128 MiB of HBM per device.

```python
import math
import jax
import jax.numpy as jnp
from jax import lax

SCAN_HEADS = 64
P_SIZE = 64
N = 128
D = 4096
FF_DEV = 768
FF = 3072
BLK = 128
CAP = 256
TOK_DEV = 1024
SEQUENCE_TOKENS = 8192
BLOCKS = 64


def draw_decay_log(key, part):
    random_subkeys = jax.random.split(key, 7)
    ranking = jax.random.permutation(random_subkeys[0], SCAN_HEADS)
    fast_count = jax.random.randint(random_subkeys[1], (), SCAN_HEADS // 4, SCAN_HEADS // 2 + 1)
    is_fast = ranking < fast_count
    fast_rate = jnp.exp(jax.random.uniform(random_subkeys[2], (SCAN_HEADS,), jnp.float32, math.log(1.0 / 50.0), math.log(1.0 / 30.0)))
    slow_rate = math.log(10.0) / (4.0 * SEQUENCE_TOKENS)
    decay_rate = jnp.where(is_fast, fast_rate, slow_rate)
    block_factor = jnp.exp(jax.random.uniform(random_subkeys[3], (SCAN_HEADS, SEQUENCE_TOKENS // BLK), jnp.float32, -math.log(2.0), math.log(2.0)))
    block_factor = jnp.repeat(block_factor, BLK, axis=1)
    token_factor = jax.random.uniform(random_subkeys[4], (SCAN_HEADS, SEQUENCE_TOKENS), jnp.float32, 0.5, 1.5)
    baseline_log = -decay_rate[:, None] * block_factor * token_factor
    spike_locations = jax.random.randint(random_subkeys[5], (SCAN_HEADS, 2), 0, SEQUENCE_TOKENS)
    spike_loss = jax.random.uniform(random_subkeys[6], (SCAN_HEADS, 2), jnp.float32, 0.2, 0.4)
    token_positions = jnp.arange(SEQUENCE_TOKENS)
    spike_log = jnp.zeros((SCAN_HEADS, SEQUENCE_TOKENS), jnp.float32)
    for spike_index in range(2):
        matched = token_positions[None, :] == spike_locations[:, spike_index:spike_index + 1]
        spike_log = spike_log + jnp.where(matched, jnp.log1p(-spike_loss[:, spike_index:spike_index + 1]), 0.0)
    return baseline_log + spike_log


def shuffled(subkey):
    return jax.random.permutation(subkey, TOK_DEV)


def draw_expert_slot(key, part):
    span_count = SEQUENCE_TOKENS // TOK_DEV
    random_subkeys = jax.random.split(key, 3)
    shifts = jax.random.randint(random_subkeys[0], (span_count,), 0, 4)
    fullest = jax.random.randint(random_subkeys[1], (), 0, span_count)
    shifts = jnp.where(jnp.arange(span_count) == fullest, 0, shifts)
    counts = CAP // jnp.left_shift(1, shifts)
    ranking = jax.vmap(shuffled)(jax.random.split(random_subkeys[2], span_count))
    slots = jnp.where(ranking < counts[:, None], ranking, CAP)
    return slots.reshape(SEQUENCE_TOKENS).astype(jnp.int32)


def touch_ends(values, key, low, high):
    extent = values.shape
    spot = [jax.random.randint(jax.random.fold_in(key, axis), (), 0, extent[axis]) for axis in range(len(extent))]
    values = values.at[tuple(spot)].set(low)
    longest = extent.index(max(extent))
    spot[longest] = (spot[longest] + 1) % extent[longest]
    return values.at[tuple(spot)].set(high)


def strengthened(drawn, rng, source, target, shards_of, factor):
    def block_of(dim):
        return (jnp.arange(drawn.shape[dim]) // (drawn.shape[dim] // shards_of)).reshape((-1,) + (1,) * (drawn.ndim - 1 - dim))

    one_side = jax.random.permutation(rng, shards_of)[block_of(target)]
    far = (block_of(target) + shards_of // 2) % shards_of
    return jnp.where((block_of(source) == one_side) | (block_of(source) == far), factor * drawn, drawn)


def steps_of(key, shape, pieces, low, top_value):
    factor_of = 1.0
    for position, parts in pieces:
        draws = jax.random.uniform(jax.random.fold_in(jax.random.fold_in(key, 6), position), (parts,), jnp.float32, low / len(pieces), top_value / len(pieces))
        factor_of = factor_of * jnp.repeat(jnp.exp(draws), shape[position] // parts).reshape((-1,) + (1,) * (len(shape) - 1 - position))
    return factor_of


def noise(key, dims, width, limit, shards=(), kind=jnp.bfloat16):
    result = jax.random.normal(key, dims, jnp.float32) * width
    if len(shards) > 0:
        result = steps_of(key, dims, shards, -0.22, 0.18) * result
    return jnp.clip(result, min=-limit, max=limit).astype(kind)


def heavy_noise(own_key, dims, scale, limit, cuts, heavy, kind=jnp.bfloat16):
    values = scale * jax.random.normal(own_key, dims, jnp.float32)
    if cuts:
        values = values * steps_of(own_key, dims, cuts, -0.22, 0.18)
    return jnp.clip(strengthened(values, jax.random.fold_in(own_key, 3), *heavy), -limit, limit).astype(kind)


def setup_inputs(seed: int = 0) -> dict:
    splits = jax.random.split(jax.random.key(seed), 14)
    mixer_input = noise(splits[0], (SEQUENCE_TOKENS, D), 1.0, 6.0, ((0, 8), (1, 4)))
    scale_exponent = touch_ends(jax.random.randint(splits[1], (BLOCKS, SCAN_HEADS), -1, 2), jax.random.fold_in(splits[1], 1), -1, 1).astype(jnp.int32)
    step_size = jnp.clip(jnp.exp(math.log(1.0) - 1.3862944 * jax.random.uniform(splits[2], (SCAN_HEADS, SEQUENCE_TOKENS), jnp.float32) ** steps_of(splits[2], (SCAN_HEADS, SEQUENCE_TOKENS), ((0, 4), (1, 8)), -0.2, 0.2)), 0.25, 1.0)
    decay_log = draw_decay_log(jax.random.fold_in(splits[13], 71), 0)
    state_input = noise(splits[4], (SEQUENCE_TOKENS, N), 1.0, 6.0, ((0, 8),))
    state_output = noise(splits[5], (SEQUENCE_TOKENS, N), N ** -0.5, 0.5, ((0, 8),))
    skip_gain = jnp.clip(0.5 + 1.0 * jax.random.uniform(splits[6], (SCAN_HEADS,), jnp.float32) ** steps_of(splits[6], (SCAN_HEADS,), ((0, 4),), -0.2, 0.2), 0.5, 1.5)
    gate_input = noise(splits[7], (SEQUENCE_TOKENS, D), 1.0, 6.0, ((0, 8), (1, 4)))
    norm_gain = jnp.clip(1.0 + 0.15 * jax.random.normal(splits[8], (D,), jnp.float32), 0.25, 1.75)
    up_weight = noise(splits[9], (D, FF), D ** -0.5, 0.09375, ((0, 8), (1, 4)))
    down_weight = heavy_noise(splits[10], (FF, D), FF ** -0.5, 0.15625, ((0, 4), (1, 8)), (0, 1, 8, 2.0))
    expert_slot = draw_expert_slot(jax.random.fold_in(splits[13], 71), 0)
    gate_prob = jnp.clip(0.2 + 0.8 * jax.random.uniform(splits[12], (SEQUENCE_TOKENS,), jnp.float32) ** steps_of(splits[12], (SEQUENCE_TOKENS,), ((0, 8),), -0.2, 0.2), 0.2, 1.0)
    return {"mixer_input": mixer_input, "scale_exponent": scale_exponent, "step_size": step_size, "decay_log": decay_log, "state_input": state_input, "state_output": state_output, "skip_gain": skip_gain, "gate_input": gate_input, "norm_gain": norm_gain, "up_weight": up_weight, "down_weight": down_weight, "expert_slot": expert_slot, "gate_prob": gate_prob}


highest = lax.Precision.HIGHEST

def reference(mixer_input, scale_exponent, step_size, decay_log, state_input, state_output, skip_gain, gate_input, norm_gain, up_weight, down_weight, expert_slot, gate_prob):
    factor = jnp.exp2(scale_exponent.astype(jnp.float32))
    x_in = mixer_input.astype(jnp.float32).reshape(BLOCKS, BLK, SCAN_HEADS, P_SIZE) * factor[:, None, :, None]
    b_blocks = state_input.astype(jnp.float32).reshape(BLOCKS, BLK, N)
    c_blocks = state_output.astype(jnp.float32).reshape(BLOCKS, BLK, N)
    step_blocks = step_size.reshape(SCAN_HEADS, BLOCKS, BLK).transpose(1, 0, 2)
    decay_blocks = decay_log.reshape(SCAN_HEADS, BLOCKS, BLK).transpose(1, 0, 2)
    causal = jnp.arange(BLK)[:, None] >= jnp.arange(BLK)[None, :]

    def advance(carry_state, block_items):
        x_block, b_block, c_block, step_block, decay_block = block_items
        cumulative = jnp.cumsum(decay_block, axis=1)
        scores = jnp.einsum('in,jn->ij', c_block, b_block, precision=highest)
        spread = jnp.where(causal, cumulative[:, :, None] - cumulative[:, None, :], -jnp.inf)
        mixing = jnp.exp(spread) * scores[None] * step_block[:, None, :]
        inner_part = jnp.einsum('hij,jhp->ihp', mixing, x_block, precision=highest)
        carried = jnp.einsum('in,hi,hnp->ihp', c_block, jnp.exp(cumulative), carry_state, precision=highest)
        tail_decay = jnp.exp(cumulative[:, -1:] - cumulative) * step_block
        block_state = jnp.einsum('hj,jn,jhp->hnp', tail_decay, b_block, x_block, precision=highest)
        new_state = jnp.exp(cumulative[:, -1])[:, None, None] * carry_state + block_state
        return (new_state, inner_part + carried)
    initial = jnp.zeros((SCAN_HEADS, N, P_SIZE), jnp.float32)
    _, mixed_out = lax.scan(advance, initial, (x_in, b_blocks, c_blocks, step_blocks, decay_blocks))
    mixer_out = (mixed_out + skip_gain[None, None, :, None] * x_in).reshape(SEQUENCE_TOKENS, SCAN_HEADS, P_SIZE)
    gated_out = mixer_out * jax.nn.silu(gate_input.astype(jnp.float32).reshape(SEQUENCE_TOKENS, SCAN_HEADS, P_SIZE))
    inverse_rms = lax.rsqrt(lax.optimization_barrier(jnp.mean(gated_out * gated_out, axis=2, keepdims=True)) + 1e-05)
    normed = (gated_out * inverse_rms * norm_gain.reshape(SCAN_HEADS, P_SIZE)).reshape(SEQUENCE_TOKENS, SCAN_HEADS * P_SIZE).astype(jnp.bfloat16)
    span_count = SEQUENCE_TOKENS // TOK_DEV
    normed_spans = normed.reshape(span_count, TOK_DEV, SCAN_HEADS * P_SIZE)
    slot_spans = expert_slot.reshape(span_count, TOK_DEV)
    group_count = FF // FF_DEV

    def expert(span_items):
        span_rows, span_slots = span_items
        places = jnp.arange(CAP, dtype=jnp.int32)[:, None] == span_slots[None, :]
        dispatched = jnp.dot(places.astype(jnp.bfloat16), span_rows, preferred_element_type=jnp.float32).astype(jnp.bfloat16)
        up_act = jnp.dot(dispatched, up_weight, preferred_element_type=jnp.float32)
        hidden = jax.nn.silu(up_act).astype(jnp.bfloat16)
        expert_out = jnp.zeros((CAP, SCAN_HEADS * P_SIZE), jnp.float32)
        for group in range(group_count):
            partial_sum = jnp.dot(hidden[:, group * FF_DEV:(group + 1) * FF_DEV], down_weight[group * FF_DEV:(group + 1) * FF_DEV, :], preferred_element_type=jnp.float32)
            expert_out = expert_out + partial_sum.astype(jnp.bfloat16).astype(jnp.float32)
        return lax.dot_general(places.astype(jnp.float32), expert_out, (((0,), (0,)), ((), ())), precision=highest)
    expert_tok = lax.map(expert, (normed_spans, slot_spans)).reshape(SEQUENCE_TOKENS, SCAN_HEADS * P_SIZE)
    return (normed.astype(jnp.float32) + gate_prob[:, None] * expert_tok).astype(jnp.bfloat16)
```

```python
import functools

import jax
import jax.numpy as jnp
from jax import lax
from jax.experimental import pallas as pl
from jax.experimental.pallas import tpu as pltpu
from jax.sharding import PartitionSpec as P

CAP = 256
SUB = 64
F32 = jnp.float32
BF16 = jnp.bfloat16
HI = lax.Precision.HIGHEST
VMEM = 60 * 1024 * 1024


def iota(shape, dim):
    return lax.broadcasted_iota(jnp.int32, shape, dim)


def contract0(a, b):
    return lax.dot_general(a, b, (((0,), (0,)), ((), ())), preferred_element_type=F32)


def split2(v):
    high = v.astype(BF16)
    return jnp.concatenate([high, (v - high.astype(F32)).astype(BF16)], axis=0)


def spread_of(heads, chans):
    return iota((heads, chans), 1) // (chans // heads) == iota((heads, chans), 0)


def lanes_of(column, spread):
    return jnp.sum(jnp.where(spread, column, 0.0), axis=0, keepdims=True)


def scale_cols(sc_ref, start, count, blk):
    rows = sc_ref.shape[0]
    hot = iota((rows, count), 0) == (start + iota((rows, count), 1)) // blk
    return contract0(jnp.exp2(sc_ref[...].astype(F32)).astype(BF16), hot.astype(BF16))


def end_kernel(x_ref, b_ref, st_ref, dl_ref, sc_ref, msg_ref, hs, ds, *, blk):
    step = pl.program_id(0)
    span, chans = x_ref.shape
    heads = st_ref.shape[0]
    states = b_ref.shape[1]

    @pl.when(step == 0)
    def _():
        hs[...] = jnp.zeros_like(hs)
        ds[...] = jnp.ones_like(ds)

    later = (iota((span, span), 0) > iota((span, span), 1)).astype(F32)
    decay = dl_ref[...]
    tail = jnp.dot(decay, later, precision=HI, preferred_element_type=F32)
    w = jnp.exp(tail) * st_ref[...] * scale_cols(sc_ref, step * span, span, blk)
    spread = spread_of(heads, chans)
    hot = spread.astype(BF16)
    wide = contract0(split2(w), jnp.concatenate([hot, hot], axis=0))
    xw = (x_ref[...].astype(F32) * wide).astype(BF16)
    keep = lanes_of(jnp.exp(jnp.sum(decay, axis=1, keepdims=True)), spread)
    hs[...] = keep * hs[...] + contract0(b_ref[...], xw)
    ds[...] = keep * ds[...]

    @pl.when(step == pl.num_programs(0) - 1)
    def _():
        msg_ref[:states, :] = hs[...].astype(BF16)
        total = ds[...]
        high = total.astype(BF16)
        low = (total - high.astype(F32)).astype(BF16)
        msg_ref[states:, :] = jnp.concatenate([high, low], axis=0)


def local_kernel(x_ref, g_ref, b_ref, c_ref, st_ref, dl_ref, sc_ref, sk_ref, a_ref, w_ref, hs, gr, *, blk):
    step = pl.program_id(0)
    span, chans = x_ref.shape
    heads = st_ref.shape[0]

    @pl.when(step == 0)
    def _():
        hs[...] = jnp.zeros_like(hs)
        gr[...] = jnp.ones_like(gr)

    decay = dl_ref[...]
    row = iota((span, span), 0)
    col = iota((span, span), 1)
    same = row // SUB == col // SUB
    upto = jnp.where(row <= col, 1.0, 0.0) - jnp.where(row % SUB < SUB // 2, 1.0, 0.0)
    rel = jnp.dot(decay, jnp.where(same, upto, 0.0), precision=HI, preferred_element_type=F32)
    scale = scale_cols(sc_ref, step * span, span, blk)
    u = jnp.exp(rel)
    v = jnp.exp(-rel) * st_ref[...] * scale
    spread = spread_of(heads, chans)
    hot = spread.astype(BF16)
    hot2 = jnp.concatenate([hot, hot], axis=0)
    u_wide = contract0(split2(u), hot2)
    v_wide = contract0(split2(v), hot2)
    skip = lanes_of(sk_ref[...] * scale[:, :1], spread)
    x = x_ref[...].astype(F32)
    xv = (x * v_wide).astype(BF16)
    b = b_ref[...]
    c = c_ref[...]
    scores = lax.dot_general(c, b, (((1,), (1,)), ((), ())), preferred_element_type=F32)
    scores = jnp.where(same & (row >= col), scores, 0.0).astype(BF16)
    place = iota((heads, span), 1)
    g = g_ref[...].astype(F32)
    gate = g / (1.0 + jnp.exp(-g))
    for part in range(span // SUB):
        lo = part * SUB
        hi = lo + SUB
        first = (place >= lo) & (place < lo + SUB // 2)
        second = (place >= lo + SUB // 2) & (place < hi)
        head_in = lanes_of(jnp.exp(jnp.sum(jnp.where(first, decay, 0.0), axis=1, keepdims=True)), spread)
        head_out = lanes_of(jnp.exp(jnp.sum(jnp.where(second, decay, 0.0), axis=1, keepdims=True)), spread)
        mid = head_in * hs[...]
        lhs = jnp.concatenate([scores[lo:hi], c[lo:hi]], axis=1)
        rhs = jnp.concatenate([xv, mid.astype(BF16)], axis=0)
        acc = jnp.dot(lhs, rhs, preferred_element_type=F32)
        hs[...] = head_out * (mid + contract0(b[lo:hi], xv[lo:hi]))
        mid_growth = head_in * gr[0:1, :]
        gr[...] = jnp.broadcast_to(head_out * mid_growth, gr.shape)
        u_part = u_wide[lo:hi]
        a_ref[lo:hi, :] = (u_part * acc + skip * x[lo:hi]) * gate[lo:hi]
        w_ref[lo:hi, :] = (u_part * mid_growth * gate[lo:hi]).astype(BF16)


def norm_kernel(c_ref, a_ref, w_ref, h_ref, gain_ref, slot_ref, n_ref, d_ref, acc, *, width):
    step = pl.program_id(0)
    span, chans = a_ref.shape
    handed = jnp.dot(c_ref[...], h_ref[...], preferred_element_type=F32)
    t = a_ref[...] + w_ref[...].astype(F32) * handed
    square = (t * t).astype(BF16)
    group = min(256, chans)
    same = iota((group, group), 0) // width == iota((group, group), 1) // width
    mean_of = jnp.where(same, 1.0 / width, 0.0).astype(BF16)
    mean = jnp.concatenate(
        [
            jnp.dot(square[:, k : k + group], mean_of, preferred_element_type=F32)
            for k in range(0, chans, group)
        ],
        axis=1,
    )
    normed = (t * lax.rsqrt(mean + 1e-05) * gain_ref[...]).astype(BF16)
    n_ref[...] = normed
    pick = (iota((CAP, span), 0) == slot_ref[...]).astype(BF16)
    rows = jnp.dot(pick, normed, preferred_element_type=F32)

    @pl.when(step == 0)
    def _():
        acc[...] = rows

    @pl.when(step > 0)
    def _():
        acc[...] = acc[...] + rows

    @pl.when(step == pl.num_programs(0) - 1)
    def _():
        d_ref[...] = acc[...].astype(BF16)


def expert_kernel(pos_ref, *refs, ring, shards):
    own = refs[0]
    ups = refs[1:ring]
    downs = refs[ring : 2 * ring - 1]
    base = 2 * ring - 1
    u_hbm = refs[base : base + shards]
    d_hbm = refs[base + shards : base + 2 * shards]
    out = refs[base + 2 * shards]
    act, u_buf, d_buf, u_sem, d_sem = refs[base + 2 * shards + 1 :]
    z = pos_ref[0]
    c = pos_ref[1]
    chans = own.shape[1]
    u_copies = [pltpu.make_async_copy(u_hbm[k], u_buf.at[k], u_sem.at[k]) for k in range(shards)]
    d_copies = [pltpu.make_async_copy(d_hbm[k], d_buf.at[k], d_sem.at[k]) for k in range(shards)]
    for copy in u_copies + d_copies:
        copy.start()
    act[z] = own[...]
    for k in range(1, ring):
        act[lax.rem(z - k + ring, ring)] = ups[k - 1][...] + downs[ring - k - 1][...]
    feats = u_buf.shape[1]
    total = jnp.zeros((own.shape[0], u_buf.shape[2]), F32)
    for k in range(shards):
        u_copies[k].wait()
        first = jnp.bitwise_xor(c, k) * feats
        a = act[first // chans, :, pl.ds(pl.multiple_of(lax.rem(first, chans), 128), feats)]
        total = total + jnp.dot(a, u_buf[k], preferred_element_type=F32)
    hidden = (total / (1.0 + jnp.exp(-total))).astype(BF16)
    cols = d_buf.shape[2]
    for k in range(shards):
        d_copies[k].wait()
        first = jnp.bitwise_xor(c, k) * cols
        term = jnp.dot(hidden, d_buf[k], preferred_element_type=F32).astype(BF16)
        out[first // chans, :, pl.ds(pl.multiple_of(lax.rem(first, chans), 128), cols)] = term


def final_kernel(pos_ref, n_ref, slot_ref, prob_ref, own_ref, up_ref, down_ref, o_ref, sums):
    @pl.when(pl.program_id(0) == 0)
    def _():
        total = own_ref[0].astype(F32) + up_ref[...].astype(F32) + down_ref[...].astype(F32)
        sums[...] = split2(total)

    span = n_ref.shape[0]
    pick = (iota((span, 2 * CAP), 1) % CAP == slot_ref[...]).astype(BF16)
    token = jnp.dot(pick, sums[...], preferred_element_type=F32)
    o_ref[...] = (n_ref[...].astype(F32) + prob_ref[...] * token).astype(BF16)


def params():
    return pltpu.CompilerParams(vmem_limit_bytes=VMEM)


def rows_spec(span, cols):
    return pl.BlockSpec((span, cols), lambda i, *_: (i, 0))


def cols_spec(rows, span):
    return pl.BlockSpec((rows, span), lambda i, *_: (0, i))


def whole(shape):
    return pl.BlockSpec(shape, lambda i, *_: (0,) * len(shape))


def gather_pieces(value, axis, count, order):
    pieces = {0: value}
    for mask in order:
        pairs = [(i, i ^ mask) for i in range(count)]
        for key in list(pieces):
            pieces[key ^ mask] = lax.ppermute(pieces[key], axis, pairs)
    return [pieces[k] for k in range(count)]


def entering_state(message, states, axis, count):
    def parts(m):
        end = m[:states].astype(F32)
        keep = m[states : states + 1].astype(F32) + m[states + 8 : states + 9].astype(F32)
        return end, keep

    def pack(end, keep):
        high = keep.astype(BF16)
        low = (keep - high.astype(F32)).astype(BF16)
        rows = (8, keep.shape[1])
        return jnp.concatenate([end.astype(BF16), jnp.broadcast_to(high, rows), jnp.broadcast_to(low, rows)], axis=0)

    index = lax.axis_index(axis)
    end, keep = parts(message)
    prior = jnp.zeros_like(end)
    before = jnp.ones_like(keep)
    mask = 1
    while mask < count:
        got_end, got_keep = parts(lax.ppermute(message, axis, [(i, i ^ mask) for i in range(count)]))
        above = (index & mask) != 0
        prior = jnp.where(above, prior + before * got_end, prior)
        before = jnp.where(above, before * got_keep, before)
        mask *= 2
        if mask < count:
            end = jnp.where(above, keep * got_end + end, got_keep * end + got_end)
            keep = keep * got_keep
            message = pack(end, keep)
    return prior.astype(BF16)


def body(ctx, ring, mixer_input, scale_exponent, step_size, decay_log, state_input, state_output, skip_gain,
         gate_input, norm_gain, up_weight, down_weight, expert_slot, gate_prob):
    tokens, chans = mixer_input.shape
    heads = skip_gain.shape[0]
    states = state_input.shape[1]
    width = chans // heads
    blk = tokens // scale_exponent.shape[0]
    position = jnp.stack([lax.axis_index("exp"), lax.axis_index("ctx")]).astype(jnp.int32)

    span = 256
    message = pl.pallas_call(
        functools.partial(end_kernel, blk=blk),
        grid=(tokens // span,),
        in_specs=[rows_spec(span, chans), rows_spec(span, states), cols_spec(heads, span), cols_spec(heads, span),
                  whole(scale_exponent.shape)],
        out_specs=whole((states + 16, chans)),
        out_shape=jax.ShapeDtypeStruct((states + 16, chans), BF16),
        scratch_shapes=[pltpu.VMEM((states, chans), F32), pltpu.VMEM((8, chans), F32)],
        compiler_params=params(),
        name="end_state",
    )(mixer_input, state_input, step_size, decay_log, scale_exponent)

    start = entering_state(message, states, "ctx", ctx)

    local, weight = pl.pallas_call(
        functools.partial(local_kernel, blk=blk),
        grid=(tokens // blk,),
        in_specs=[rows_spec(blk, chans), rows_spec(blk, chans), rows_spec(blk, states), rows_spec(blk, states),
                  cols_spec(heads, blk), cols_spec(heads, blk), whole(scale_exponent.shape), whole((heads, 1))],
        out_specs=[rows_spec(blk, chans), rows_spec(blk, chans)],
        out_shape=[jax.ShapeDtypeStruct((tokens, chans), F32), jax.ShapeDtypeStruct((tokens, chans), BF16)],
        scratch_shapes=[pltpu.VMEM((states, chans), F32), pltpu.VMEM((8, chans), F32)],
        compiler_params=params(),
        name="local_out",
    )(mixer_input, gate_input, state_input, state_output, step_size, decay_log, scale_exponent,
      skip_gain[:, None])

    normed, dispatched = pl.pallas_call(
        functools.partial(norm_kernel, width=width),
        grid=(tokens // span,),
        in_specs=[rows_spec(span, states), rows_spec(span, chans), rows_spec(span, chans), whole((states, chans)),
                  whole((1, chans)), cols_spec(1, span)],
        out_specs=[rows_spec(span, chans), whole((CAP, chans))],
        out_shape=[jax.ShapeDtypeStruct((tokens, chans), BF16), jax.ShapeDtypeStruct((CAP, chans), BF16)],
        scratch_shapes=[pltpu.VMEM((CAP, chans), F32)],
        compiler_params=params(),
        name="norm_dispatch",
    )(state_output, local, weight, start, norm_gain[None], expert_slot[None])

    masks = []
    mask = 2
    while mask < ctx:
        masks.append(mask)
        mask *= 2
    ups = gather_pieces(up_weight, "ctx", ctx, masks + [1])
    downs = gather_pieces(down_weight, "ctx", ctx, masks[::-1] + [1])

    rise = [(i, i + 1) for i in range(ring - 1)]
    fall = [(i + 1, i) for i in range(ring - 1)]
    from_low = []
    from_high = []
    low = high = dispatched
    for _ in range(ring - 1):
        low = lax.ppermute(low, "exp", rise)
        high = lax.ppermute(high, "exp", fall)
        from_low.append(low)
        from_high.append(high)

    any_spec = pl.BlockSpec(memory_space=pl.ANY)
    terms = pl.pallas_call(
        functools.partial(expert_kernel, ring=ring, shards=ctx),
        grid_spec=pltpu.PrefetchScalarGridSpec(
            num_scalar_prefetch=1,
            grid=(1,),
            in_specs=[whole((CAP, chans))] * (2 * ring - 1) + [any_spec] * (2 * ctx),
            out_specs=whole((ring, CAP, chans)),
            scratch_shapes=[
                pltpu.VMEM((ring, CAP, chans), BF16),
                pltpu.VMEM((ctx,) + up_weight.shape, BF16),
                pltpu.VMEM((ctx,) + down_weight.shape, BF16),
                pltpu.SemaphoreType.DMA((ctx,)),
                pltpu.SemaphoreType.DMA((ctx,)),
            ],
        ),
        out_shape=jax.ShapeDtypeStruct((ring, CAP, chans), BF16),
        compiler_params=params(),
        name="expert",
    )(position, dispatched, *from_low, *from_high, *ups, *downs)

    z = position[0]
    up_sum = down_sum = None
    for turn in range(1, ring):
        far = lax.dynamic_index_in_dim(terms, (z + ring - turn) % ring, 0, keepdims=False)
        near = lax.dynamic_index_in_dim(terms, (z + turn) % ring, 0, keepdims=False)
        if turn > 1:
            far = (far.astype(F32) + up_sum.astype(F32)).astype(BF16)
            near = (near.astype(F32) + down_sum.astype(F32)).astype(BF16)
        up_sum = lax.ppermute(far, "exp", [(i, i + 1) for i in range(min(turn, ring - 1))])
        down_sum = lax.ppermute(near, "exp", [(i, i - 1) for i in range(max(ring - turn, 1), ring)])

    return pl.pallas_call(
        final_kernel,
        grid_spec=pltpu.PrefetchScalarGridSpec(
            num_scalar_prefetch=1,
            grid=(tokens // span,),
            in_specs=[rows_spec(span, chans), rows_spec(span, 1), rows_spec(span, 1),
                      pl.BlockSpec((1, CAP, chans), lambda i, pos: (pos[0], 0, 0)),
                      whole((CAP, chans)), whole((CAP, chans))],
            out_specs=rows_spec(span, chans),
            scratch_shapes=[pltpu.VMEM((2 * CAP, chans), BF16)],
        ),
        out_shape=jax.ShapeDtypeStruct((tokens, chans), BF16),
        compiler_params=params(),
        name="combine",
    )(position, normed, expert_slot[:, None], gate_prob[:, None], terms, up_sum, down_sum)


def solution(mesh):
    in_specs = (
        P("ctx", "exp"),
        P("ctx", "exp"),
        P("exp", "ctx"),
        P("exp", "ctx"),
        P("ctx", None),
        P("ctx", None),
        P("exp"),
        P("ctx", "exp"),
        P("exp"),
        P("ctx", "exp"),
        P("exp", "ctx"),
        P("ctx"),
        P("ctx"),
    )
    run = functools.partial(body, mesh.shape["ctx"], mesh.shape["exp"])
    return jax.shard_map(run, mesh=mesh, in_specs=in_specs, out_specs=P("ctx", "exp"), check_vma=False)
```

```python
import functools

import jax
import jax.numpy as jnp
from jax import lax
from jax.experimental import pallas as pl
from jax.experimental.pallas import tpu as pltpu
from jax.sharding import PartitionSpec as P


CAP = 256
SUB = 64
F32 = jnp.float32
BF16 = jnp.bfloat16
HI = lax.Precision.HIGHEST
VMEM = 60 * 1024 * 1024


def iota(shape, dim):
    return lax.broadcasted_iota(jnp.int32, shape, dim)


def contract0(a, b):
    return lax.dot_general(a, b, (((0,), (0,)), ((), ())), preferred_element_type=F32)


def split2(v):
    high = v.astype(BF16)
    return jnp.concatenate([high, (v - high.astype(F32)).astype(BF16)], axis=0)


def spread_of(heads, chans):
    return iota((heads, chans), 1) // (chans // heads) == iota((heads, chans), 0)


def lanes_of(column, spread):
    return jnp.sum(jnp.where(spread, column, 0.0), axis=0, keepdims=True)


def scale_cols(sc_ref, start, count, blk):
    rows = sc_ref.shape[0]
    hot = iota((rows, count), 0) == (start + iota((rows, count), 1)) // blk
    return contract0(jnp.exp2(sc_ref[...].astype(F32)).astype(BF16), hot.astype(BF16))


def end_kernel(x_ref, b_ref, st_ref, dl_ref, sc_ref, msg_ref, hs, ds, *, blk):
    step = pl.program_id(0)
    span, chans = x_ref.shape
    heads = st_ref.shape[0]
    states = b_ref.shape[1]

    @pl.when(step == 0)
    def _():
        hs[...] = jnp.zeros_like(hs)
        ds[...] = jnp.ones_like(ds)

    later = (iota((span, span), 0) > iota((span, span), 1)).astype(F32)
    decay = dl_ref[...]
    tail = jnp.dot(decay, later, precision=HI, preferred_element_type=F32)
    w = jnp.exp(tail) * st_ref[...] * scale_cols(sc_ref, step * span, span, blk)
    spread = spread_of(heads, chans)
    hot = spread.astype(BF16)
    wide = contract0(split2(w), jnp.concatenate([hot, hot], axis=0))
    xw = (x_ref[...].astype(F32) * wide).astype(BF16)
    keep = lanes_of(jnp.exp(jnp.sum(decay, axis=1, keepdims=True)), spread)
    hs[...] = keep * hs[...] + contract0(b_ref[...], xw)
    ds[...] = keep * ds[...]

    @pl.when(step == pl.num_programs(0) - 1)
    def _():
        msg_ref[:states, :] = hs[...].astype(BF16)
        total = ds[...]
        high = total.astype(BF16)
        low = (total - high.astype(F32)).astype(BF16)
        msg_ref[states:, :] = jnp.concatenate([high, low], axis=0)


def local_kernel(x_ref, g_ref, b_ref, c_ref, st_ref, dl_ref, sc_ref, sk_ref, a_ref, w_ref, hs, gr, *, blk):
    step = pl.program_id(0)
    span, chans = x_ref.shape
    heads = st_ref.shape[0]

    @pl.when(step == 0)
    def _():
        hs[...] = jnp.zeros_like(hs)
        gr[...] = jnp.ones_like(gr)

    decay = dl_ref[...]
    row = iota((span, span), 0)
    col = iota((span, span), 1)
    same = row // SUB == col // SUB
    upto = jnp.where(row <= col, 1.0, 0.0) - jnp.where(row % SUB < SUB // 2, 1.0, 0.0)
    rel = jnp.dot(decay, jnp.where(same, upto, 0.0), precision=HI, preferred_element_type=F32)
    scale = scale_cols(sc_ref, step * span, span, blk)
    u = jnp.exp(rel)
    v = jnp.exp(-rel) * st_ref[...] * scale
    spread = spread_of(heads, chans)
    hot = spread.astype(BF16)
    hot2 = jnp.concatenate([hot, hot], axis=0)
    u_wide = contract0(split2(u), hot2)
    v_wide = contract0(split2(v), hot2)
    skip = lanes_of(turned(sk_ref[...]) * scale[:, :1], spread)
    x = x_ref[...].astype(F32)
    xv = (x * v_wide).astype(BF16)
    b = b_ref[...]
    c = c_ref[...]
    scores = lax.dot_general(c, b, (((1,), (1,)), ((), ())), preferred_element_type=F32)
    scores = jnp.where(same & (row >= col), scores, 0.0).astype(BF16)
    place = iota((heads, span), 1)
    g = g_ref[...].astype(F32)
    gate = g / (1.0 + jnp.exp(-g))
    for part in range(span // SUB):
        lo = part * SUB
        hi = lo + SUB
        first = (place >= lo) & (place < lo + SUB // 2)
        second = (place >= lo + SUB // 2) & (place < hi)
        head_in = lanes_of(jnp.exp(jnp.sum(jnp.where(first, decay, 0.0), axis=1, keepdims=True)), spread)
        head_out = lanes_of(jnp.exp(jnp.sum(jnp.where(second, decay, 0.0), axis=1, keepdims=True)), spread)
        mid = head_in * hs[...]
        lhs = jnp.concatenate([scores[lo:hi], c[lo:hi]], axis=1)
        rhs = jnp.concatenate([xv, mid.astype(BF16)], axis=0)
        acc = jnp.dot(lhs, rhs, preferred_element_type=F32)
        hs[...] = head_out * (mid + contract0(b[lo:hi], xv[lo:hi]))
        mid_growth = head_in * gr[0:1, :]
        gr[...] = jnp.broadcast_to(head_out * mid_growth, gr.shape)
        u_part = u_wide[lo:hi]
        a_ref[lo:hi, :] = (u_part * acc + skip * x[lo:hi]) * gate[lo:hi]
        w_ref[lo:hi, :] = (u_part * mid_growth * gate[lo:hi]).astype(BF16)


def norm_kernel(c_ref, a_ref, w_ref, h_ref, gain_ref, slot_ref, n_ref, *outs, width):
    d_refs, acc = outs[:-1], outs[-1]
    step = pl.program_id(0)
    span, chans = a_ref.shape
    handed = jnp.dot(c_ref[...], h_ref[...], preferred_element_type=F32)
    t = a_ref[...] + w_ref[...].astype(F32) * handed
    square = (t * t).astype(BF16)
    group = min(256, chans)
    same = iota((group, group), 0) // width == iota((group, group), 1) // width
    mean_of = jnp.where(same, 1.0 / width, 0.0).astype(BF16)
    mean = jnp.concatenate(
        [
            jnp.dot(square[:, k : k + group], mean_of, preferred_element_type=F32)
            for k in range(0, chans, group)
        ],
        axis=1,
    )
    normed = (t * lax.rsqrt(mean + 1e-05) * gain_ref[...]).astype(BF16)
    n_ref[...] = normed
    pick = (iota((CAP, span), 0) == slot_ref[...]).astype(BF16)
    rows = jnp.dot(pick, normed, preferred_element_type=F32)

    @pl.when(step == 0)
    def _():
        acc[...] = rows

    @pl.when(step > 0)
    def _():
        acc[...] = acc[...] + rows

    @pl.when(step == pl.num_programs(0) - 1)
    def _():
        rows = CAP // len(d_refs)
        for k, d_ref in enumerate(d_refs):
            d_ref[...] = acc[k * rows : (k + 1) * rows, :].astype(BF16)


def turned(row):
    return jnp.broadcast_to(row, (8, row.shape[1])).T[:, :1]


def expert_kernel(*refs, ring, shards, groups):
    inputs = refs[: sum(groups)]
    u_hbm = refs[sum(groups) : sum(groups) + shards]
    d_hbm = refs[sum(groups) + shards : sum(groups) + 2 * shards]
    outs = refs[sum(groups) + 2 * shards : sum(groups) + 2 * shards + ring]
    act, terms, u_buf, d_buf, u_sem, d_sem = refs[sum(groups) + 2 * shards + ring :]
    z = lax.axis_index("exp")
    c = lax.axis_index("ctx")
    rows, chans = inputs[0].shape
    u_copies = [pltpu.make_async_copy(u_hbm[k], u_buf.at[k], u_sem.at[k]) for k in range(shards)]
    d_copies = [pltpu.make_async_copy(d_hbm[k], d_buf.at[k], d_sem.at[k]) for k in range(shards)]
    for copy in u_copies + d_copies:
        copy.start()
    at = 0
    for k in range(ring):
        piece = inputs[at][...]
        for other in range(at + 1, at + groups[k]):
            piece = piece + inputs[other][...]
        act[k] = piece
        at += groups[k]
    feats = u_buf.shape[1]
    total = jnp.zeros((rows, u_buf.shape[2]), F32)
    for k in range(shards):
        u_copies[k].wait()
        first = jnp.bitwise_xor(c, k) * feats
        a = act[jnp.bitwise_xor(z, first // chans), :, pl.ds(pl.multiple_of(lax.rem(first, chans), 128), feats)]
        total = total + jnp.dot(a, u_buf[k], preferred_element_type=F32)
    hidden = (total / (1.0 + jnp.exp(-total))).astype(BF16)
    cols = d_buf.shape[2]
    for k in range(shards):
        d_copies[k].wait()
        first = jnp.bitwise_xor(c, k) * cols
        term = jnp.dot(hidden, d_buf[k], preferred_element_type=F32).astype(BF16)
        terms[jnp.bitwise_xor(z, first // chans), :, pl.ds(pl.multiple_of(lax.rem(first, chans), 128), cols)] = term
    for k in range(ring):
        outs[k][...] = terms[k]


def final_kernel(*refs, parts):
    n_ref, slot_ref, prob_ref = refs[:3]
    terms = refs[3:-2]
    o_ref, sums = refs[-2:]

    @pl.when(pl.program_id(0) == 0)
    def _():
        each = len(terms) // parts
        rows = CAP // parts
        for k in range(parts):
            total = terms[k * each][...].astype(F32)
            for other in range(k * each + 1, (k + 1) * each):
                total = total + terms[other][...].astype(F32)
            high = total.astype(BF16)
            sums[k * rows : (k + 1) * rows, :] = high
            sums[CAP + k * rows : CAP + (k + 1) * rows, :] = (total - high.astype(F32)).astype(BF16)

    span = n_ref.shape[0]
    slot = turned(slot_ref[...].astype(F32)).astype(jnp.int32)
    pick = (iota((span, 2 * CAP), 1) % CAP == slot).astype(BF16)
    token = jnp.dot(pick, sums[...], preferred_element_type=F32)
    o_ref[...] = (n_ref[...].astype(F32) + turned(prob_ref[...]) * token).astype(BF16)


def params():
    return pltpu.CompilerParams(vmem_limit_bytes=VMEM)


def rows_spec(span, cols):
    return pl.BlockSpec((span, cols), lambda i, *_: (i, 0))


def cols_spec(rows, span):
    return pl.BlockSpec((rows, span), lambda i, *_: (0, i))


def whole(shape):
    return pl.BlockSpec(shape, lambda i, *_: (0,) * len(shape))


def swap(value, axis, count, mask):
    return lax.ppermute(value, axis, [(i, i ^ mask) for i in range(count)])


def gather_pieces(value, axis, count, order):
    pieces = {0: value}
    if count == 8:
        far, near = order
        pieces[far] = swap(value, axis, count, far)
        pieces[near] = swap(value, axis, count, near)
        pieces[6] = swap(pieces[far], axis, count, near)
        for key in (0, far, near, 6):
            pieces[key ^ 1] = swap(pieces[key], axis, count, 1)
    else:
        mask = 1
        while mask < count:
            for key in list(pieces):
                pieces[key ^ mask] = swap(pieces[key], axis, count, mask)
            mask *= 2
    return [pieces[k] for k in range(count)]


ENDS = [(0, 1), (3, 2)]
MIDDLE = [(1, 2), (2, 1)]
OUTWARD = [(1, 0), (2, 3)]


def gather_line(own, ring):
    if ring != 4:
        return [own] + [swap(own, "exp", ring, k) for k in range(1, ring)], [1] * ring
    beside = swap(own, "exp", ring, 1)
    cross = lax.ppermute(own, "exp", MIDDLE)
    cross_far = lax.ppermute(beside, "exp", MIDDLE)
    out_near = lax.ppermute(cross, "exp", OUTWARD)
    out_far = lax.ppermute(cross_far, "exp", OUTWARD)
    return [own, beside, cross_far, out_near, cross, out_far], [1, 1, 2, 2]


def added(a, b):
    return (a.astype(F32) + b.astype(F32)).astype(BF16)


def sum_line(terms, ring):
    if ring != 4:
        return [terms[0]] + [swap(terms[k], "exp", ring, k) for k in range(1, ring)]
    far = lax.ppermute(terms[3], "exp", ENDS)
    near = lax.ppermute(terms[2], "exp", ENDS)
    far = lax.ppermute(added(terms[2], far), "exp", MIDDLE)
    near = lax.ppermute(added(terms[3], near), "exp", MIDDLE)
    beside = swap(added(terms[1], far), "exp", ring, 1)
    return [terms[0], near, beside]


def entering_state(message, states, axis, count):
    def parts(m):
        end = m[:states].astype(F32)
        keep = m[states : states + 1].astype(F32) + m[states + 8 : states + 9].astype(F32)
        return end, keep

    def pack(end, keep):
        high = keep.astype(BF16)
        low = (keep - high.astype(F32)).astype(BF16)
        rows = (8, keep.shape[1])
        return jnp.concatenate([end.astype(BF16), jnp.broadcast_to(high, rows), jnp.broadcast_to(low, rows)], axis=0)

    index = lax.axis_index(axis)
    end, keep = parts(message)
    prior = jnp.zeros_like(end)
    before = jnp.ones_like(keep)
    mask = 1
    while mask < count:
        got_end, got_keep = parts(swap(message, axis, count, mask))
        above = (index & mask) != 0
        prior = jnp.where(above, prior + before * got_end, prior)
        before = jnp.where(above, before * got_keep, before)
        mask *= 2
        if mask < count:
            end = jnp.where(above, keep * got_end + end, got_keep * end + got_end)
            keep = keep * got_keep
            message = pack(end, keep)
    return prior.astype(BF16)


def body(ctx, ring, mixer_input, scale_exponent, step_size, decay_log, state_input, state_output, skip_gain,
         gate_input, norm_gain, up_weight, down_weight, expert_slot, gate_prob):
    tokens, chans = mixer_input.shape
    heads = skip_gain.shape[0]
    states = state_input.shape[1]
    width = chans // heads
    blk = tokens // scale_exponent.shape[0]
    parts = 2
    rows = CAP // parts

    span = 256
    message = pl.pallas_call(
        functools.partial(end_kernel, blk=blk),
        grid=(tokens // span,),
        in_specs=[rows_spec(span, chans), rows_spec(span, states), cols_spec(heads, span), cols_spec(heads, span),
                  whole(scale_exponent.shape)],
        out_specs=whole((states + 16, chans)),
        out_shape=jax.ShapeDtypeStruct((states + 16, chans), BF16),
        scratch_shapes=[pltpu.VMEM((states, chans), F32), pltpu.VMEM((8, chans), F32)],
        compiler_params=params(),
        name="end_state",
    )(mixer_input, state_input, step_size, decay_log, scale_exponent)

    start = entering_state(message, states, "ctx", ctx)

    local, weight = pl.pallas_call(
        functools.partial(local_kernel, blk=blk),
        grid=(tokens // blk,),
        in_specs=[rows_spec(blk, chans), rows_spec(blk, chans), rows_spec(blk, states), rows_spec(blk, states),
                  cols_spec(heads, blk), cols_spec(heads, blk), whole(scale_exponent.shape), whole((1, heads))],
        out_specs=[rows_spec(blk, chans), rows_spec(blk, chans)],
        out_shape=[jax.ShapeDtypeStruct((tokens, chans), F32), jax.ShapeDtypeStruct((tokens, chans), BF16)],
        scratch_shapes=[pltpu.VMEM((states, chans), F32), pltpu.VMEM((8, chans), F32)],
        compiler_params=params(),
        name="local_out",
    )(mixer_input, gate_input, state_input, state_output, step_size, decay_log, scale_exponent,
      skip_gain[None])

    normed, *dispatched = pl.pallas_call(
        functools.partial(norm_kernel, width=width),
        grid=(tokens // span,),
        in_specs=[rows_spec(span, states), rows_spec(span, chans), rows_spec(span, chans), whole((states, chans)),
                  whole((1, chans)), cols_spec(1, span)],
        out_specs=[rows_spec(span, chans)] + [whole((rows, chans))] * parts,
        out_shape=[jax.ShapeDtypeStruct((tokens, chans), BF16)] + [jax.ShapeDtypeStruct((rows, chans), BF16)] * parts,
        scratch_shapes=[pltpu.VMEM((CAP, chans), F32)],
        compiler_params=params(),
        name="norm_dispatch",
    )(state_output, local, weight, start, norm_gain[None], expert_slot[None])

    ups = gather_pieces(up_weight, "ctx", ctx, (2, 4))
    downs = gather_pieces(down_weight, "ctx", ctx, (4, 2))

    any_spec = pl.BlockSpec(memory_space=pl.ANY)
    summed = []
    for part in range(parts):
        pieces, groups = gather_line(dispatched[part], ring)
        terms = pl.pallas_call(
            functools.partial(expert_kernel, ring=ring, shards=ctx, groups=groups),
            in_specs=[whole((rows, chans))] * len(pieces) + [any_spec] * (2 * ctx),
            out_specs=[whole((rows, chans))] * ring,
            grid=(1,),
            scratch_shapes=[
                pltpu.VMEM((ring, rows, chans), BF16),
                pltpu.VMEM((ring, rows, chans), BF16),
                pltpu.VMEM((ctx,) + up_weight.shape, BF16),
                pltpu.VMEM((ctx,) + down_weight.shape, BF16),
                pltpu.SemaphoreType.DMA((ctx,)),
                pltpu.SemaphoreType.DMA((ctx,)),
            ],
            out_shape=[jax.ShapeDtypeStruct((rows, chans), BF16)] * ring,
            compiler_params=params(),
        )(*pieces, *ups, *downs)
        summed += sum_line(terms, ring)

    return pl.pallas_call(
        functools.partial(final_kernel, parts=parts),
        grid=(tokens // span,),
        in_specs=[rows_spec(span, chans), cols_spec(1, span), cols_spec(1, span)]
        + [whole((rows, chans))] * len(summed),
        out_specs=rows_spec(span, chans),
        scratch_shapes=[pltpu.VMEM((2 * CAP, chans), BF16)],
        out_shape=jax.ShapeDtypeStruct((tokens, chans), BF16),
        compiler_params=params(),
        name="combine",
    )(normed, expert_slot[None], gate_prob[None], *summed)


def solution(mesh):
    in_specs = (
        P("ctx", "exp"),
        P("ctx", "exp"),
        P("exp", "ctx"),
        P("exp", "ctx"),
        P("ctx", None),
        P("ctx", None),
        P("exp"),
        P("ctx", "exp"),
        P("exp"),
        P("ctx", "exp"),
        P("exp", "ctx"),
        P("ctx"),
        P("ctx"),
    )
    ctx, ring = mesh.shape["ctx"], mesh.shape["exp"]

    def run(*arrays):
        return body(ctx, ring, *arrays)

    return jax.shard_map(run, mesh=mesh, in_specs=in_specs, out_specs=P("ctx", "exp"), check_vma=False)
```

```python
import functools

import jax
import jax.numpy as jnp
from jax import lax
from jax.experimental import pallas as pl
from jax.experimental.pallas import tpu as pltpu
from jax.sharding import PartitionSpec as P


CAP = 256
SUB = 64
F32 = jnp.float32
BF16 = jnp.bfloat16
HI = lax.Precision.HIGHEST
MIB = 1024 * 1024


def iota(shape, dim):
    return lax.broadcasted_iota(jnp.int32, shape, dim)


def contract0(a, b):
    return lax.dot_general(a, b, (((0,), (0,)), ((), ())), preferred_element_type=F32)


def split2(v):
    high = v.astype(BF16)
    return jnp.concatenate([high, (v - high.astype(F32)).astype(BF16)], axis=0)


def spread_of(heads, chans):
    return iota((heads, chans), 1) // (chans // heads) == iota((heads, chans), 0)


def lanes_of(column, spread):
    return jnp.sum(jnp.where(spread, column, 0.0), axis=0, keepdims=True)


def scale_cols(sc_ref, start, count, blk):
    rows = sc_ref.shape[0]
    hot = iota((rows, count), 0) == (start + iota((rows, count), 1)) // blk
    return contract0(jnp.exp2(sc_ref[...].astype(F32)).astype(BF16), hot.astype(BF16))


def end_kernel(x_ref, b_ref, st_ref, dl_ref, sc_ref, msg_ref, hs, ds, *, blk):
    step = pl.program_id(0)
    span, chans = x_ref.shape
    heads = st_ref.shape[0]
    states = b_ref.shape[1]

    @pl.when(step == 0)
    def _():
        hs[...] = jnp.zeros_like(hs)
        ds[...] = jnp.ones_like(ds)

    later = (iota((span, span), 0) > iota((span, span), 1)).astype(F32)
    decay = dl_ref[...]
    tail = jnp.dot(decay, later, precision=HI, preferred_element_type=F32)
    w = jnp.exp(tail) * st_ref[...] * scale_cols(sc_ref, step * span, span, blk)
    spread = spread_of(heads, chans)
    hot = spread.astype(BF16)
    wide = contract0(split2(w), jnp.concatenate([hot, hot], axis=0))
    xw = (x_ref[...].astype(F32) * wide).astype(BF16)
    keep = lanes_of(jnp.exp(jnp.sum(decay, axis=1, keepdims=True)), spread)
    hs[...] = keep * hs[...] + contract0(b_ref[...], xw)
    ds[...] = keep * ds[...]

    @pl.when(step == pl.num_programs(0) - 1)
    def _():
        msg_ref[:states, :] = hs[...].astype(BF16)
        total = ds[...]
        high = total.astype(BF16)
        low = (total - high.astype(F32)).astype(BF16)
        msg_ref[states:, :] = jnp.concatenate([high, low], axis=0)


def local_kernel(x_ref, g_ref, b_ref, c_ref, st_ref, dl_ref, sc_ref, sk_ref, a_ref, w_ref, hs, gr, *, blk):
    step = pl.program_id(0)
    span, chans = x_ref.shape
    heads = st_ref.shape[0]

    @pl.when(step == 0)
    def _():
        hs[...] = jnp.zeros_like(hs)
        gr[...] = jnp.ones_like(gr)

    decay = dl_ref[...]
    row = iota((span, span), 0)
    col = iota((span, span), 1)
    same = row // SUB == col // SUB
    upto = jnp.where(row <= col, 1.0, 0.0) - jnp.where(row % SUB < SUB // 2, 1.0, 0.0)
    rel = jnp.dot(decay, jnp.where(same, upto, 0.0), precision=HI, preferred_element_type=F32)
    scale = scale_cols(sc_ref, step * span, span, blk)
    u = jnp.exp(rel)
    v = jnp.exp(-rel) * st_ref[...] * scale
    spread = spread_of(heads, chans)
    hot = spread.astype(BF16)
    hot2 = jnp.concatenate([hot, hot], axis=0)
    u_wide = contract0(split2(u), hot2)
    v_wide = contract0(split2(v), hot2)
    skip = lanes_of(turned(sk_ref[...]) * scale[:, :1], spread)
    x = x_ref[...].astype(F32)
    xv = (x * v_wide).astype(BF16)
    b = b_ref[...]
    c = c_ref[...]
    scores = lax.dot_general(c, b, (((1,), (1,)), ((), ())), preferred_element_type=F32)
    scores = jnp.where(same & (row >= col), scores, 0.0).astype(BF16)
    place = iota((heads, span), 1)
    g = g_ref[...].astype(F32)
    gate = g / (1.0 + jnp.exp(-g))
    for part in range(span // SUB):
        lo = part * SUB
        hi = lo + SUB
        first = (place >= lo) & (place < lo + SUB // 2)
        second = (place >= lo + SUB // 2) & (place < hi)
        head_in = lanes_of(jnp.exp(jnp.sum(jnp.where(first, decay, 0.0), axis=1, keepdims=True)), spread)
        head_out = lanes_of(jnp.exp(jnp.sum(jnp.where(second, decay, 0.0), axis=1, keepdims=True)), spread)
        mid = head_in * hs[...]
        lhs = jnp.concatenate([scores[lo:hi], c[lo:hi]], axis=1)
        rhs = jnp.concatenate([xv, mid.astype(BF16)], axis=0)
        acc = jnp.dot(lhs, rhs, preferred_element_type=F32)
        hs[...] = head_out * (mid + contract0(b[lo:hi], xv[lo:hi]))
        mid_growth = head_in * gr[0:1, :]
        gr[...] = jnp.broadcast_to(head_out * mid_growth, gr.shape)
        u_part = u_wide[lo:hi]
        a_ref[lo:hi, :] = (u_part * acc + skip * x[lo:hi]) * gate[lo:hi]
        w_ref[lo:hi, :] = (u_part * mid_growth * gate[lo:hi]).astype(BF16)


def turned(row):
    return jnp.broadcast_to(row, (8, row.shape[1])).T[:, :1]


def keep_of(ref, lanes=slice(None)):
    rows = ref.shape[0]
    return ref[rows - 16 : rows - 15, lanes].astype(F32) + ref[rows - 8 : rows - 7, lanes].astype(F32)


def chip_kernel(own_ref, other_ref, o_ref):
    core = lax.rem(lax.axis_index("ctx"), 2)
    states = own_ref.shape[0] - 16
    half = o_ref.shape[1]
    lanes = pl.ds(pl.multiple_of(core * half, 128), half)
    own = own_ref[:states, lanes].astype(F32)
    other = other_ref[:states, lanes].astype(F32)
    own_keep = keep_of(own_ref, lanes)
    other_keep = keep_of(other_ref, lanes)
    total = jnp.where(core == 0, other_keep * own + other, own_keep * other + own)
    keep = own_keep * other_keep
    o_ref[:states, :] = total.astype(BF16)
    high = keep.astype(BF16)
    low = (keep - high.astype(F32)).astype(BF16)
    o_ref[states : states + 8, :] = jnp.broadcast_to(high, (8, half))
    o_ref[states + 8 :, :] = jnp.broadcast_to(low, (8, half))


def prior_kernel(*refs):
    o_ref = refs[-1]
    chip = lax.axis_index("ctx") // 2
    states = o_ref.shape[0]
    chips = [jnp.bitwise_xor(chip, k + 1) for k in range(len(refs) - 1)]
    keeps = [keep_of(ref) for ref in refs[:-1]]
    total = jnp.zeros(o_ref.shape, F32)
    for k, ref in enumerate(refs[:-1]):
        weight = jnp.ones_like(keeps[k])
        for other, keep in zip(chips, keeps):
            weight = jnp.where((other > chips[k]) & (other < chip), weight * keep, weight)
        weight = jnp.where(chips[k] < chip, weight, jnp.zeros_like(weight))
        total = total + weight * ref[:states, :].astype(F32)
    o_ref[...] = total.astype(BF16)


def norm_kernel(flip_ref, c_ref, a_ref, w_ref, gain_ref, slot_ref, h_ref, *refs, width):
    n_ref, d_ref, acc, start = refs[-4:]
    step = pl.program_id(0)
    span, half = a_ref.shape

    @pl.when(step == 0)
    def _():
        acc[...] = jnp.zeros_like(acc)
        if len(refs) > 4:
            prior = h_ref[...].astype(F32)
            states = prior.shape[0]
            before = keep_of(refs[0]) * prior + refs[0][:states, :].astype(F32)
            start[...] = jnp.where(flip_ref[0] == 1, before, prior).astype(BF16)
        else:
            start[...] = h_ref[...]

    group = min(256, half)
    same = iota((group, group), 0) // width == iota((group, group), 1) // width
    mean_of = jnp.where(same, 1.0 / width, 0.0).astype(BF16)
    for k in range(0, half, group):
        for r in range(0, span, 128):
            handed = jnp.dot(c_ref[r : r + 128, :], start[:, k : k + group], preferred_element_type=F32)
            t = a_ref[r : r + 128, k : k + group] + w_ref[r : r + 128, k : k + group].astype(F32) * handed
            mean = jnp.dot((t * t).astype(BF16), mean_of, preferred_element_type=F32)
            normed = t * lax.rsqrt(mean + 1e-05) * gain_ref[:, k : k + group]
            n_ref[r : r + 128, k : k + group] = normed.astype(BF16)
    pick = (iota((CAP, span), 0) == slot_ref[...]).astype(BF16)
    acc[...] = acc[...] + jnp.dot(pick, n_ref[...], preferred_element_type=F32)

    @pl.when(step == pl.num_programs(0) - 1)
    def _():
        d_ref[...] = acc[...].astype(BF16)


def expert_kernel(flip_ref, *refs, ring, shards, groups, half):
    halves = len(groups)
    count = sum(map(sum, groups))
    inputs = refs[:count]
    hbm = refs[count : count + 2 * shards]
    outs = refs[count + 2 * shards : count + 2 * shards + ring]
    act, terms, u_buf, d_buf, sem = refs[count + 2 * shards + ring :]
    z = lax.axis_index("exp")
    c = lax.axis_index("ctx")
    rows = inputs[0].shape[0]
    chans = half * halves
    copies = [pltpu.make_async_copy(hbm[k], u_buf.at[k], sem.at[k]) for k in range(shards)]
    copies += [pltpu.make_async_copy(hbm[shards + k], d_buf.at[k], sem.at[shards + k]) for k in range(shards)]
    ahead = min(3, len(copies))
    for copy in copies[:ahead]:
        copy.start()

    def ready(index):
        if index + ahead < len(copies):
            copies[index + ahead].start()
        copies[index].wait()

    at = 0
    for q in range(halves):
        lanes = pl.ds(pl.multiple_of(jnp.bitwise_xor(flip_ref[0], q) * half, 128), half)
        for k in range(ring):
            piece = inputs[at][...]
            for other in range(at + 1, at + groups[q][k]):
                piece = piece + inputs[other][...]
            act[k, :, lanes] = piece
            at += groups[q][k]
    feats = u_buf.shape[1]
    total = jnp.zeros((rows, u_buf.shape[2]), F32)
    for k in range(shards):
        ready(k)
        first = jnp.bitwise_xor(c, k) * feats
        a = act[jnp.bitwise_xor(z, first // chans), :, pl.ds(pl.multiple_of(lax.rem(first, chans), 128), feats)]
        total = total + jnp.dot(a, u_buf[k], preferred_element_type=F32)
    hidden = (total / (1.0 + jnp.exp(-total))).astype(BF16)
    cols = d_buf.shape[2]
    for k in range(shards):
        ready(shards + k)
        first = jnp.bitwise_xor(c, k) * cols
        term = jnp.dot(hidden, d_buf[k], preferred_element_type=F32).astype(BF16)
        terms[jnp.bitwise_xor(z, first // chans), :, pl.ds(pl.multiple_of(lax.rem(first, chans), 128), cols)] = term
    for k in range(ring):
        outs[k][...] = terms[k]


def final_kernel(flip_ref, slot_ref, prob_ref, *refs, base, count):
    rests = refs[:count]
    terms = refs[count:-2]
    o_ref, sums = refs[-2:]
    rows = sums.shape[0]

    @pl.when(pl.program_id(0) == 0)
    def _():
        total = terms[0][...].astype(F32)
        for other in terms[1:]:
            total = total + other[...].astype(F32)
        sums[...] = total.astype(BF16)

    span = o_ref.shape[0]
    slot = turned(slot_ref[...].astype(F32)).astype(jnp.int32)
    prob = turned(prob_ref[...])
    pick = (iota((span, rows), 1) + base == slot).astype(BF16)
    part = o_ref.shape[1] // count
    for q in range(count):
        lanes = slice(None)
        if count > 1:
            lanes = pl.ds(pl.multiple_of(jnp.bitwise_xor(flip_ref[0], q) * part, 128), part)
        token = jnp.dot(pick, sums[:, lanes], preferred_element_type=F32)
        o_ref[:, lanes] = (rests[q][...].astype(F32) + prob * token).astype(BF16)


def params(size=16):
    return pltpu.CompilerParams(vmem_limit_bytes=size * MIB)


def rows_spec(span, cols):
    return pl.BlockSpec((span, cols), lambda i, *_: (i, 0))


def cols_spec(rows, span):
    return pl.BlockSpec((rows, span), lambda i, *_: (0, i))


def whole(shape):
    return pl.BlockSpec(shape, lambda i, *_: (0,) * len(shape))


def swap(value, axis, count, mask):
    return lax.ppermute(value, axis, [(i, i ^ mask) for i in range(count)])


def gather_pieces(value, axis, count, order):
    pieces = {0: value}
    if count == 8:
        far, near = order
        pieces[far] = swap(value, axis, count, far)
        pieces[near] = swap(value, axis, count, near)
        pieces[6] = swap(pieces[far], axis, count, near)
        for key in (0, far, near, 6):
            pieces[key ^ 1] = swap(pieces[key], axis, count, 1)
    else:
        mask = 1
        while mask < count:
            for key in list(pieces):
                pieces[key ^ mask] = swap(pieces[key], axis, count, mask)
            mask *= 2
    return [pieces[k] for k in range(count)]


ENDS = [(0, 1), (3, 2)]
MIDDLE = [(1, 2), (2, 1)]
OUTWARD = [(1, 0), (2, 3)]


def gather_line(own, ring):
    if ring != 4:
        return [own] + [swap(own, "exp", ring, k) for k in range(1, ring)], [1] * ring
    beside = swap(own, "exp", ring, 1)
    cross = lax.ppermute(own, "exp", MIDDLE)
    cross_far = lax.ppermute(beside, "exp", MIDDLE)
    out_near = lax.ppermute(cross, "exp", OUTWARD)
    out_far = lax.ppermute(cross_far, "exp", OUTWARD)
    return [own, beside, cross_far, out_near, cross, out_far], [1, 1, 2, 2]


def added(a, b):
    return (a.astype(F32) + b.astype(F32)).astype(BF16)


def sum_line(terms, ring):
    if ring != 4:
        return [terms[0]] + [swap(terms[k], "exp", ring, k) for k in range(1, ring)]
    far = lax.ppermute(terms[3], "exp", ENDS)
    near = lax.ppermute(terms[2], "exp", ENDS)
    far = lax.ppermute(added(terms[2], far), "exp", MIDDLE)
    near = lax.ppermute(added(terms[3], near), "exp", MIDDLE)
    beside = swap(added(terms[1], far), "exp", ring, 1)
    return [terms[0], near, beside]


def entering_state(message, states, axis, count):
    def parts(m):
        end = m[:states].astype(F32)
        keep = m[states : states + 1].astype(F32) + m[states + 8 : states + 9].astype(F32)
        return end, keep

    def pack(end, keep):
        high = keep.astype(BF16)
        low = (keep - high.astype(F32)).astype(BF16)
        rows = (8, keep.shape[1])
        return jnp.concatenate([end.astype(BF16), jnp.broadcast_to(high, rows), jnp.broadcast_to(low, rows)], axis=0)

    index = lax.axis_index(axis)
    end, keep = parts(message)
    prior = jnp.zeros_like(end)
    before = jnp.ones_like(keep)
    mask = 1
    while mask < count:
        got_end, got_keep = parts(swap(message, axis, count, mask))
        above = (index & mask) != 0
        prior = jnp.where(above, prior + before * got_end, prior)
        before = jnp.where(above, before * got_keep, before)
        mask *= 2
        if mask < count:
            end = jnp.where(above, keep * got_end + end, got_keep * end + got_end)
            keep = keep * got_keep
            message = pack(end, keep)
    return prior.astype(BF16)


def body(ctx, ring, mixer_input, scale_exponent, step_size, decay_log, state_input, state_output, skip_gain,
         gate_input, norm_gain, up_weight, down_weight, expert_slot, gate_prob):
    tokens, chans = mixer_input.shape
    heads = skip_gain.shape[0]
    states = state_input.shape[1]
    width = chans // heads
    blk = tokens // scale_exponent.shape[0]
    halves = parts = 2
    half = chans // halves
    rows = CAP // parts
    paired = ctx == 8
    flip = lax.rem(lax.axis_index("ctx"), 2)[None] if paired else jnp.zeros((1,), jnp.int32)

    span = 256
    message = pl.pallas_call(
        functools.partial(end_kernel, blk=blk),
        grid=(tokens // span,),
        in_specs=[rows_spec(span, chans), rows_spec(span, states), cols_spec(heads, span), cols_spec(heads, span),
                  whole(scale_exponent.shape)],
        out_specs=whole((states + 16, chans)),
        out_shape=jax.ShapeDtypeStruct((states + 16, chans), BF16),
        scratch_shapes=[pltpu.VMEM((states, chans), F32), pltpu.VMEM((8, chans), F32)],
        compiler_params=params(),
        name="end_state",
    )(mixer_input, state_input, step_size, decay_log, scale_exponent)

    if paired:
        beside = swap(message, "ctx", ctx, 1)
        chip_shape = jax.ShapeDtypeStruct((states + 16, half), BF16)
        chip = pl.pallas_call(
            chip_kernel, out_shape=chip_shape, compiler_params=params(), name="chip_state"
        )(message, beside)
        chips = [swap(chip, "ctx", ctx, mask) for mask in (2, 4, 6)]
        prior = pl.pallas_call(
            prior_kernel,
            out_shape=jax.ShapeDtypeStruct((states, half), BF16),
            compiler_params=params(),
            name="prior",
        )(*chips)
        priors = [prior, swap(prior, "ctx", ctx, 1)]
    else:
        start = entering_state(message, states, "ctx", ctx)

    local, weight = pl.pallas_call(
        functools.partial(local_kernel, blk=blk),
        grid=(tokens // blk,),
        in_specs=[rows_spec(blk, chans), rows_spec(blk, chans), rows_spec(blk, states), rows_spec(blk, states),
                  cols_spec(heads, blk), cols_spec(heads, blk), whole(scale_exponent.shape), whole((1, heads))],
        out_specs=[rows_spec(blk, chans), rows_spec(blk, chans)],
        out_shape=[jax.ShapeDtypeStruct((tokens, chans), F32), jax.ShapeDtypeStruct((tokens, chans), BF16)],
        scratch_shapes=[pltpu.VMEM((states, chans), F32), pltpu.VMEM((8, chans), F32)],
        compiler_params=params(),
        name="local_out",
    )(mixer_input, gate_input, state_input, state_output, step_size, decay_log, scale_exponent,
      skip_gain[None])

    normed = []
    dispatched = []
    for q in range(halves):

        def col(i, flip, q=q):
            return (0, jnp.bitwise_xor(flip[0], q))

        def block(i, flip, q=q):
            return (i, jnp.bitwise_xor(flip[0], q))

        if paired:
            entry = [whole((states, half)), pl.BlockSpec((states + 16, half), col)]
            values = [priors[q], beside]
        else:
            entry = [pl.BlockSpec((states, half), col)]
            values = [start]
        outs = pl.pallas_call(
            functools.partial(norm_kernel, width=width),
            grid_spec=pltpu.PrefetchScalarGridSpec(
                num_scalar_prefetch=1,
                grid=(tokens // span,),
                in_specs=[rows_spec(span, states), pl.BlockSpec((span, half), block), pl.BlockSpec((span, half), block),
                          pl.BlockSpec((1, half), col), cols_spec(1, span)] + entry,
                out_specs=[rows_spec(span, half), whole((CAP, half))],
                scratch_shapes=[pltpu.VMEM((CAP, half), F32), pltpu.VMEM((states, half), BF16)],
            ),
            out_shape=[jax.ShapeDtypeStruct((tokens, half), BF16), jax.ShapeDtypeStruct((CAP, half), BF16)],
            compiler_params=params(),
        )(flip, state_output, local, weight, norm_gain[None], expert_slot[None], *values)
        normed.append(outs[0])
        dispatched.append(outs[1])

    ups = gather_pieces(up_weight, "ctx", ctx, (2, 4))
    downs = gather_pieces(down_weight, "ctx", ctx, (4, 2))

    pieces = []
    groups = []
    for q in range(halves):
        got, group = gather_line(dispatched[q], ring)
        pieces += got
        groups.append(group)

    any_spec = pl.BlockSpec(memory_space=pl.ANY)
    rests = normed
    summed = []
    for part in range(parts):
        terms = pl.pallas_call(
            functools.partial(expert_kernel, ring=ring, shards=ctx, groups=groups, half=half),
            grid_spec=pltpu.PrefetchScalarGridSpec(
                num_scalar_prefetch=1,
                grid=(1,),
                in_specs=[pl.BlockSpec((rows, half), lambda i, flip, part=part: (part, 0))] * len(pieces)
                + [any_spec] * (2 * ctx),
                out_specs=[whole((rows, chans))] * ring,
                scratch_shapes=[
                    pltpu.VMEM((ring, rows, chans), BF16),
                    pltpu.VMEM((ring, rows, chans), BF16),
                    pltpu.VMEM((ctx,) + up_weight.shape, BF16),
                    pltpu.VMEM((ctx,) + down_weight.shape, BF16),
                    pltpu.SemaphoreType.DMA((2 * ctx,)),
                ],
            ),
            out_shape=[jax.ShapeDtypeStruct((rows, chans), BF16)] * ring,
            compiler_params=params(26),
        )(flip, *pieces, *ups, *downs)
        summed.append(sum_line(terms, ring))

    for part in range(parts):
        rests = [pl.pallas_call(
            functools.partial(final_kernel, base=part * rows, count=len(rests)),
            grid_spec=pltpu.PrefetchScalarGridSpec(
                num_scalar_prefetch=1,
                grid=(tokens // span,),
                in_specs=[cols_spec(1, span), cols_spec(1, span)]
                + [rows_spec(span, chans // len(rests))] * len(rests)
                + [whole((rows, chans))] * len(summed[part]),
                out_specs=rows_spec(span, chans),
                scratch_shapes=[pltpu.VMEM((rows, chans), BF16)],
            ),
            out_shape=jax.ShapeDtypeStruct((tokens, chans), BF16),
            compiler_params=params(),
        )(flip, expert_slot[None], gate_prob[None], *rests, *summed[part])]
    return rests[0]


def solution(mesh):
    in_specs = (
        P("ctx", "exp"),
        P("ctx", "exp"),
        P("exp", "ctx"),
        P("exp", "ctx"),
        P("ctx", None),
        P("ctx", None),
        P("exp"),
        P("ctx", "exp"),
        P("exp"),
        P("ctx", "exp"),
        P("exp", "ctx"),
        P("ctx"),
        P("ctx"),
    )
    ctx, ring = mesh.shape["ctx"], mesh.shape["exp"]

    def run(*arrays):
        return body(ctx, ring, *arrays)

    return jax.shard_map(run, mesh=mesh, in_specs=in_specs, out_specs=P("ctx", "exp"), check_vma=False)
```

```python
import functools

import jax
import jax.numpy as jnp
from jax import lax
from jax.experimental import pallas as pl
from jax.experimental.pallas import tpu as pltpu
from jax.sharding import PartitionSpec as P


CAP = 256
SUB = 64
F32 = jnp.float32
BF16 = jnp.bfloat16
HI = lax.Precision.HIGHEST
MIB = 1024 * 1024


def iota(shape, dim):
    return lax.broadcasted_iota(jnp.int32, shape, dim)


def contract0(a, b):
    return lax.dot_general(a, b, (((0,), (0,)), ((), ())), preferred_element_type=F32)


def split2(v):
    high = v.astype(BF16)
    return jnp.concatenate([high, (v - high.astype(F32)).astype(BF16)], axis=0)


def spread_of(heads, chans):
    return iota((heads, chans), 1) // (chans // heads) == iota((heads, chans), 0)


def lanes_of(column, spread):
    return jnp.sum(jnp.where(spread, column, 0.0), axis=0, keepdims=True)


def scale_cols(sc_ref, start, count, blk):
    rows = sc_ref.shape[0]
    hot = iota((rows, count), 0) == (start + iota((rows, count), 1)) // blk
    return contract0(jnp.exp2(sc_ref[...].astype(F32)).astype(BF16), hot.astype(BF16))


def end_kernel(x_ref, b_ref, st_ref, dl_ref, sc_ref, msg_ref, hs, ds, *, blk):
    step = pl.program_id(0)
    span, chans = x_ref.shape
    heads = st_ref.shape[0]
    states = b_ref.shape[1]

    @pl.when(step == 0)
    def _():
        hs[...] = jnp.zeros_like(hs)
        ds[...] = jnp.ones_like(ds)

    later = (iota((span, span), 0) > iota((span, span), 1)).astype(F32)
    decay = dl_ref[...]
    tail = jnp.dot(decay, later, precision=HI, preferred_element_type=F32)
    w = jnp.exp(tail) * st_ref[...] * scale_cols(sc_ref, step * span, span, blk)
    spread = spread_of(heads, chans)
    hot = spread.astype(BF16)
    wide = contract0(split2(w), jnp.concatenate([hot, hot], axis=0))
    xw = (x_ref[...].astype(F32) * wide).astype(BF16)
    keep = lanes_of(jnp.exp(jnp.sum(decay, axis=1, keepdims=True)), spread)
    hs[...] = keep * hs[...] + contract0(b_ref[...], xw)
    ds[...] = keep * ds[...]

    @pl.when(step == pl.num_programs(0) - 1)
    def _():
        msg_ref[:states, :] = hs[...].astype(BF16)
        total = ds[...]
        high = total.astype(BF16)
        low = (total - high.astype(F32)).astype(BF16)
        msg_ref[states:, :] = jnp.concatenate([high, low], axis=0)


def local_kernel(x_ref, g_ref, b_ref, c_ref, st_ref, dl_ref, sc_ref, sk_ref, a_ref, w_ref, hs, gr, *, blk):
    step = pl.program_id(0)
    span, chans = x_ref.shape
    heads = st_ref.shape[0]

    @pl.when(step == 0)
    def _():
        hs[...] = jnp.zeros_like(hs)
        gr[...] = jnp.ones_like(gr)

    decay = dl_ref[...]
    row = iota((span, span), 0)
    col = iota((span, span), 1)
    same = row // SUB == col // SUB
    upto = jnp.where(row <= col, 1.0, 0.0) - jnp.where(row % SUB < SUB // 2, 1.0, 0.0)
    rel = jnp.dot(decay, jnp.where(same, upto, 0.0), precision=HI, preferred_element_type=F32)
    scale = scale_cols(sc_ref, step * span, span, blk)
    u = jnp.exp(rel)
    v = jnp.exp(-rel) * st_ref[...] * scale
    spread = spread_of(heads, chans)
    hot = spread.astype(BF16)
    hot2 = jnp.concatenate([hot, hot], axis=0)
    u_wide = contract0(split2(u), hot2)
    v_wide = contract0(split2(v), hot2)
    skip = lanes_of(turned(sk_ref[...]) * scale[:, :1], spread)
    x = x_ref[...].astype(F32)
    xv = (x * v_wide).astype(BF16)
    b = b_ref[...]
    c = c_ref[...]
    scores = lax.dot_general(c, b, (((1,), (1,)), ((), ())), preferred_element_type=F32)
    scores = jnp.where(same & (row >= col), scores, 0.0).astype(BF16)
    place = iota((heads, span), 1)
    g = g_ref[...].astype(F32)
    gate = 0.5 * g
    gate = gate + gate * jnp.tanh(gate)
    for part in range(span // SUB):
        lo = part * SUB
        hi = lo + SUB
        first = (place >= lo) & (place < lo + SUB // 2)
        second = (place >= lo + SUB // 2) & (place < hi)
        head_in = lanes_of(jnp.exp(jnp.sum(jnp.where(first, decay, 0.0), axis=1, keepdims=True)), spread)
        head_out = lanes_of(jnp.exp(jnp.sum(jnp.where(second, decay, 0.0), axis=1, keepdims=True)), spread)
        mid = head_in * hs[...]
        lhs = jnp.concatenate([scores[lo:hi], c[lo:hi]], axis=1)
        rhs = jnp.concatenate([xv, mid.astype(BF16)], axis=0)
        acc = jnp.dot(lhs, rhs, preferred_element_type=F32)
        hs[...] = head_out * (mid + contract0(b[lo:hi], xv[lo:hi]))
        mid_growth = head_in * gr[0:1, :]
        gr[...] = jnp.broadcast_to(head_out * mid_growth, gr.shape)
        u_gate = u_wide[lo:hi] * gate[lo:hi]
        a_ref[lo:hi, :] = (u_gate * acc + skip * x[lo:hi] * gate[lo:hi]).astype(BF16)
        w_ref[lo:hi, :] = (u_gate * mid_growth).astype(BF16)


def turned(row):
    return jnp.broadcast_to(row, (8, row.shape[1])).T[:, :1]


def keep_of(ref, lanes=slice(None)):
    rows = ref.shape[0]
    return ref[rows - 16 : rows - 15, lanes].astype(F32) + ref[rows - 8 : rows - 7, lanes].astype(F32)


def chip_kernel(own_ref, other_ref, o_ref):
    core = lax.rem(lax.axis_index("ctx"), 2)
    states = own_ref.shape[0] - 16
    half = o_ref.shape[1]
    lanes = pl.ds(pl.multiple_of(core * half, 128), half)
    own = own_ref[:states, lanes].astype(F32)
    other = other_ref[:states, lanes].astype(F32)
    own_keep = keep_of(own_ref, lanes)
    other_keep = keep_of(other_ref, lanes)
    total = jnp.where(core == 0, other_keep * own + other, own_keep * other + own)
    keep = own_keep * other_keep
    o_ref[:states, :] = total.astype(BF16)
    high = keep.astype(BF16)
    low = (keep - high.astype(F32)).astype(BF16)
    o_ref[states : states + 8, :] = jnp.broadcast_to(high, (8, half))
    o_ref[states + 8 :, :] = jnp.broadcast_to(low, (8, half))


def prior_kernel(*refs):
    o_ref = refs[-1]
    chip = lax.axis_index("ctx") // 2
    states = o_ref.shape[0]
    chips = [jnp.bitwise_xor(chip, k + 1) for k in range(len(refs) - 1)]
    keeps = [keep_of(ref) for ref in refs[:-1]]
    total = jnp.zeros(o_ref.shape, F32)
    for k, ref in enumerate(refs[:-1]):
        weight = jnp.ones_like(keeps[k])
        for other, keep in zip(chips, keeps):
            weight = jnp.where((other > chips[k]) & (other < chip), weight * keep, weight)
        weight = jnp.where(chips[k] < chip, weight, jnp.zeros_like(weight))
        total = total + weight * ref[:states, :].astype(F32)
    o_ref[...] = total.astype(BF16)


def norm_kernel(flip_ref, c_ref, a_ref, w_ref, gain_ref, slot_ref, h_ref, *refs, width):
    n_ref, d_ref, acc, start = refs[-4:]
    step = pl.program_id(0)
    span, half = a_ref.shape

    @pl.when(step == 0)
    def _():
        acc[...] = jnp.zeros_like(acc)
        if len(refs) > 4:
            prior = h_ref[...].astype(F32)
            states = prior.shape[0]
            before = keep_of(refs[0]) * prior + refs[0][:states, :].astype(F32)
            start[...] = jnp.where(flip_ref[0] == 1, before, prior).astype(BF16)
        else:
            start[...] = h_ref[...]

    group = min(256, half)
    same = iota((group, group), 0) // width == iota((group, group), 1) // width
    mean_of = jnp.where(same, 1.0 / width, 0.0).astype(BF16)
    for k in range(0, half, group):
        for r in range(0, span, 128):
            handed = jnp.dot(c_ref[r : r + 128, :], start[:, k : k + group], preferred_element_type=F32)
            t = a_ref[r : r + 128, k : k + group].astype(F32) + w_ref[r : r + 128, k : k + group].astype(F32) * handed
            mean = jnp.dot((t * t).astype(BF16), mean_of, preferred_element_type=F32)
            normed = t * lax.rsqrt(mean + 1e-05) * gain_ref[:, k : k + group]
            n_ref[r : r + 128, k : k + group] = normed.astype(BF16)
    pick = (iota((CAP, span), 0) == slot_ref[...]).astype(BF16)
    acc[...] = acc[...] + jnp.dot(pick, n_ref[...], preferred_element_type=F32)

    @pl.when(step == pl.num_programs(0) - 1)
    def _():
        d_ref[...] = acc[...].astype(BF16)


def expert_kernel(flip_ref, *refs, ring, shards, groups, half):
    halves = len(groups)
    count = sum(map(sum, groups))
    inputs = refs[:count]
    hbm = refs[count : count + 2 * shards]
    outs = refs[count + 2 * shards : count + 2 * shards + ring]
    act, terms, u_buf, d_buf, sem = refs[count + 2 * shards + ring :]
    z = lax.axis_index("exp")
    c = lax.axis_index("ctx")
    rows = inputs[0].shape[0]
    chans = half * halves
    copies = [pltpu.make_async_copy(hbm[k], u_buf.at[k], sem.at[k]) for k in range(shards)]
    copies += [pltpu.make_async_copy(hbm[shards + k], d_buf.at[k], sem.at[shards + k]) for k in range(shards)]
    ahead = min(3, len(copies))
    for copy in copies[:ahead]:
        copy.start()

    def ready(index):
        if index + ahead < len(copies):
            copies[index + ahead].start()
        copies[index].wait()

    at = 0
    for q in range(halves):
        lanes = pl.ds(pl.multiple_of(jnp.bitwise_xor(flip_ref[0], q) * half, 128), half)
        for k in range(ring):
            piece = inputs[at][...]
            for other in range(at + 1, at + groups[q][k]):
                piece = piece + inputs[other][...]
            act[k, :, lanes] = piece
            at += groups[q][k]
    feats = u_buf.shape[1]
    total = jnp.zeros((rows, u_buf.shape[2]), F32)
    for k in range(shards):
        ready(k)
        first = jnp.bitwise_xor(c, k) * feats
        a = act[jnp.bitwise_xor(z, first // chans), :, pl.ds(pl.multiple_of(lax.rem(first, chans), 128), feats)]
        total = total + jnp.dot(a, u_buf[k], preferred_element_type=F32)
    hidden = (total / (1.0 + jnp.exp(-total))).astype(BF16)
    cols = d_buf.shape[2]
    for k in range(shards):
        ready(shards + k)
        first = jnp.bitwise_xor(c, k) * cols
        term = jnp.dot(hidden, d_buf[k], preferred_element_type=F32).astype(BF16)
        terms[jnp.bitwise_xor(z, first // chans), :, pl.ds(pl.multiple_of(lax.rem(first, chans), 128), cols)] = term
    for k in range(ring):
        outs[k][...] = terms[k]


def final_kernel(flip_ref, slot_ref, prob_ref, *refs, base, count):
    rests = refs[:count]
    terms = refs[count:-2]
    o_ref, sums = refs[-2:]
    rows = sums.shape[0]

    @pl.when(pl.program_id(0) == 0)
    def _():
        total = terms[0][...].astype(F32)
        for other in terms[1:]:
            total = total + other[...].astype(F32)
        sums[...] = total.astype(BF16)

    span = o_ref.shape[0]
    slot = turned(slot_ref[...].astype(F32)).astype(jnp.int32)
    prob = turned(prob_ref[...])
    pick = (iota((span, rows), 1) + base == slot).astype(BF16)
    part = o_ref.shape[1] // count
    for q in range(count):
        lanes = slice(None)
        if count > 1:
            lanes = pl.ds(pl.multiple_of(jnp.bitwise_xor(flip_ref[0], q) * part, 128), part)
        token = jnp.dot(pick, sums[:, lanes], preferred_element_type=F32)
        o_ref[:, lanes] = (rests[q][...].astype(F32) + prob * token).astype(BF16)


def params(size=16):
    return pltpu.CompilerParams(vmem_limit_bytes=size * MIB)


def rows_spec(span, cols):
    return pl.BlockSpec((span, cols), lambda i, *_: (i, 0))


def cols_spec(rows, span):
    return pl.BlockSpec((rows, span), lambda i, *_: (0, i))


def whole(shape):
    return pl.BlockSpec(shape, lambda i, *_: (0,) * len(shape))


def swap(value, axis, count, mask):
    return lax.ppermute(value, axis, [(i, i ^ mask) for i in range(count)])


def gather_pieces(value, axis, count, order):
    pieces = {0: value}
    if count == 8:
        far, near = order
        pieces[far] = swap(value, axis, count, far)
        pieces[near] = swap(value, axis, count, near)
        pieces[6] = swap(pieces[far], axis, count, near)
        for key in (0, far, near, 6):
            pieces[key ^ 1] = swap(pieces[key], axis, count, 1)
    else:
        mask = 1
        while mask < count:
            for key in list(pieces):
                pieces[key ^ mask] = swap(pieces[key], axis, count, mask)
            mask *= 2
    return [pieces[k] for k in range(count)]


ENDS = [(0, 1), (3, 2)]
MIDDLE = [(1, 2), (2, 1)]
OUTWARD = [(1, 0), (2, 3)]


def gather_line(own, ring):
    if ring != 4:
        return [own] + [swap(own, "exp", ring, k) for k in range(1, ring)], [1] * ring
    beside = swap(own, "exp", ring, 1)
    cross = lax.ppermute(own, "exp", MIDDLE)
    cross_far = lax.ppermute(beside, "exp", MIDDLE)
    out_near = lax.ppermute(cross, "exp", OUTWARD)
    out_far = lax.ppermute(cross_far, "exp", OUTWARD)
    return [own, beside, cross_far, out_near, cross, out_far], [1, 1, 2, 2]


def added(a, b):
    return (a.astype(F32) + b.astype(F32)).astype(BF16)


def sum_line(terms, ring):
    if ring != 4:
        return [terms[0]] + [swap(terms[k], "exp", ring, k) for k in range(1, ring)]
    far = lax.ppermute(terms[3], "exp", ENDS)
    near = lax.ppermute(terms[2], "exp", ENDS)
    far = lax.ppermute(added(terms[2], far), "exp", MIDDLE)
    near = lax.ppermute(added(terms[3], near), "exp", MIDDLE)
    beside = swap(added(terms[1], far), "exp", ring, 1)
    return [terms[0], near, beside]


def entering_state(message, states, axis, count):
    def parts(m):
        end = m[:states].astype(F32)
        keep = m[states : states + 1].astype(F32) + m[states + 8 : states + 9].astype(F32)
        return end, keep

    def pack(end, keep):
        high = keep.astype(BF16)
        low = (keep - high.astype(F32)).astype(BF16)
        rows = (8, keep.shape[1])
        return jnp.concatenate([end.astype(BF16), jnp.broadcast_to(high, rows), jnp.broadcast_to(low, rows)], axis=0)

    index = lax.axis_index(axis)
    end, keep = parts(message)
    prior = jnp.zeros_like(end)
    before = jnp.ones_like(keep)
    mask = 1
    while mask < count:
        got_end, got_keep = parts(swap(message, axis, count, mask))
        above = (index & mask) != 0
        prior = jnp.where(above, prior + before * got_end, prior)
        before = jnp.where(above, before * got_keep, before)
        mask *= 2
        if mask < count:
            end = jnp.where(above, keep * got_end + end, got_keep * end + got_end)
            keep = keep * got_keep
            message = pack(end, keep)
    return prior.astype(BF16)


def body(ctx, ring, mixer_input, scale_exponent, step_size, decay_log, state_input, state_output, skip_gain,
         gate_input, norm_gain, up_weight, down_weight, expert_slot, gate_prob):
    tokens, chans = mixer_input.shape
    heads = skip_gain.shape[0]
    states = state_input.shape[1]
    width = chans // heads
    blk = tokens // scale_exponent.shape[0]
    halves = parts = 2
    half = chans // halves
    rows = CAP // parts
    paired = ctx == 8
    flip = lax.rem(lax.axis_index("ctx"), 2)[None] if paired else jnp.zeros((1,), jnp.int32)

    span = 256
    message = pl.pallas_call(
        functools.partial(end_kernel, blk=blk),
        grid=(tokens // span,),
        in_specs=[rows_spec(span, chans), rows_spec(span, states), cols_spec(heads, span), cols_spec(heads, span),
                  whole(scale_exponent.shape)],
        out_specs=whole((states + 16, chans)),
        out_shape=jax.ShapeDtypeStruct((states + 16, chans), BF16),
        scratch_shapes=[pltpu.VMEM((states, chans), F32), pltpu.VMEM((8, chans), F32)],
        compiler_params=params(60),
        name="end_state",
    )(mixer_input, state_input, step_size, decay_log, scale_exponent)

    if paired:
        beside = swap(message, "ctx", ctx, 1)
        chip_shape = jax.ShapeDtypeStruct((states + 16, half), BF16)
        chip = pl.pallas_call(
            chip_kernel, out_shape=chip_shape, compiler_params=params(), name="chip_state"
        )(message, beside)
        chips = [swap(chip, "ctx", ctx, mask) for mask in (2, 4, 6)]
        prior = pl.pallas_call(
            prior_kernel,
            out_shape=jax.ShapeDtypeStruct((states, half), BF16),
            compiler_params=params(),
            name="prior",
        )(*chips)
        priors = [prior, swap(prior, "ctx", ctx, 1)]
    else:
        start = entering_state(message, states, "ctx", ctx)

    local, weight = pl.pallas_call(
        functools.partial(local_kernel, blk=blk),
        grid=(tokens // blk,),
        in_specs=[rows_spec(blk, chans), rows_spec(blk, chans), rows_spec(blk, states), rows_spec(blk, states),
                  cols_spec(heads, blk), cols_spec(heads, blk), whole(scale_exponent.shape), whole((1, heads))],
        out_specs=[rows_spec(blk, chans), rows_spec(blk, chans)],
        out_shape=[jax.ShapeDtypeStruct((tokens, chans), BF16)] * 2,
        scratch_shapes=[pltpu.VMEM((states, chans), F32), pltpu.VMEM((8, chans), F32)],
        compiler_params=params(48),
        name="local_out",
    )(mixer_input, gate_input, state_input, state_output, step_size, decay_log, scale_exponent,
      skip_gain[None])

    normed = []
    dispatched = []
    for q in range(halves):

        def col(i, flip, q=q):
            return (0, jnp.bitwise_xor(flip[0], q))

        def block(i, flip, q=q):
            return (i, jnp.bitwise_xor(flip[0], q))

        if paired:
            entry = [whole((states, half)), pl.BlockSpec((states + 16, half), col)]
            values = [priors[q], beside]
        else:
            entry = [pl.BlockSpec((states, half), col)]
            values = [start]
        outs = pl.pallas_call(
            functools.partial(norm_kernel, width=width),
            grid_spec=pltpu.PrefetchScalarGridSpec(
                num_scalar_prefetch=1,
                grid=(tokens // span,),
                in_specs=[rows_spec(span, states), pl.BlockSpec((span, half), block), pl.BlockSpec((span, half), block),
                          pl.BlockSpec((1, half), col), cols_spec(1, span)] + entry,
                out_specs=[rows_spec(span, half), whole((CAP, half))],
                scratch_shapes=[pltpu.VMEM((CAP, half), F32), pltpu.VMEM((states, half), BF16)],
            ),
            out_shape=[jax.ShapeDtypeStruct((tokens, half), BF16), jax.ShapeDtypeStruct((CAP, half), BF16)],
            compiler_params=params(),
        )(flip, state_output, local, weight, norm_gain[None], expert_slot[None], *values)
        normed.append(outs[0])
        dispatched.append(outs[1])

    ups = gather_pieces(up_weight, "ctx", ctx, (2, 4))
    downs = gather_pieces(down_weight, "ctx", ctx, (4, 2))

    pieces = []
    groups = []
    for q in range(halves):
        got, group = gather_line(dispatched[q], ring)
        pieces += got
        groups.append(group)

    any_spec = pl.BlockSpec(memory_space=pl.ANY)
    rests = normed
    summed = []
    for part in range(parts):
        terms = pl.pallas_call(
            functools.partial(expert_kernel, ring=ring, shards=ctx, groups=groups, half=half),
            grid_spec=pltpu.PrefetchScalarGridSpec(
                num_scalar_prefetch=1,
                grid=(1,),
                in_specs=[pl.BlockSpec((rows, half), lambda i, flip, part=part: (part, 0))] * len(pieces)
                + [any_spec] * (2 * ctx),
                out_specs=[whole((rows, chans))] * ring,
                scratch_shapes=[
                    pltpu.VMEM((ring, rows, chans), BF16),
                    pltpu.VMEM((ring, rows, chans), BF16),
                    pltpu.VMEM((ctx,) + up_weight.shape, BF16),
                    pltpu.VMEM((ctx,) + down_weight.shape, BF16),
                    pltpu.SemaphoreType.DMA((2 * ctx,)),
                ],
            ),
            out_shape=[jax.ShapeDtypeStruct((rows, chans), BF16)] * ring,
            compiler_params=params(26),
        )(flip, *pieces, *ups, *downs)
        summed.append(sum_line(terms, ring))

    for part in range(parts):
        rests = [pl.pallas_call(
            functools.partial(final_kernel, base=part * rows, count=len(rests)),
            grid_spec=pltpu.PrefetchScalarGridSpec(
                num_scalar_prefetch=1,
                grid=(tokens // span,),
                in_specs=[cols_spec(1, span), cols_spec(1, span)]
                + [rows_spec(span, chans // len(rests))] * len(rests)
                + [whole((rows, chans))] * len(summed[part]),
                out_specs=rows_spec(span, chans),
                scratch_shapes=[pltpu.VMEM((rows, chans), BF16)],
            ),
            out_shape=jax.ShapeDtypeStruct((tokens, chans), BF16),
            compiler_params=params(),
        )(flip, expert_slot[None], gate_prob[None], *rests, *summed[part])]
    return rests[0]


def solution(mesh):
    in_specs = (
        P("ctx", "exp"),
        P("ctx", "exp"),
        P("exp", "ctx"),
        P("exp", "ctx"),
        P("ctx", None),
        P("ctx", None),
        P("exp"),
        P("ctx", "exp"),
        P("exp"),
        P("ctx", "exp"),
        P("exp", "ctx"),
        P("ctx"),
        P("ctx"),
    )
    ctx, ring = mesh.shape["ctx"], mesh.shape["exp"]

    def run(*arrays):
        return body(ctx, ring, *arrays)

    return jax.shard_map(run, mesh=mesh, in_specs=in_specs, out_specs=P("ctx", "exp"), check_vma=False)
```

```python
import functools

import jax
import jax.numpy as jnp
from jax import lax
from jax.experimental import pallas as pl
from jax.experimental.pallas import tpu as pltpu
from jax.sharding import PartitionSpec as P


CAP = 256
SUB = 64
F32 = jnp.float32
BF16 = jnp.bfloat16
MIB = 1024 * 1024


def iota(shape, dim):
    return lax.broadcasted_iota(jnp.int32, shape, dim)


def contract0(a, b):
    return lax.dot_general(a, b, (((0,), (0,)), ((), ())), preferred_element_type=F32)


def split2(v):
    high = v.astype(BF16)
    return jnp.concatenate([high, (v - high.astype(F32)).astype(BF16)], axis=0)


def summed_over(decay, pattern):
    heads = decay.shape[0]
    high = decay.astype(BF16)
    rest = decay - high.astype(F32)
    middle = rest.astype(BF16)
    low = (rest - middle.astype(F32)).astype(BF16)
    total = jnp.dot(jnp.concatenate([high, middle, low], axis=0), pattern, preferred_element_type=F32)
    return total[:heads] + total[heads : 2 * heads] + total[2 * heads :]


def spread_of(heads, chans):
    return iota((heads, chans), 1) // (chans // heads) == iota((heads, chans), 0)


def lanes_of(column, spread):
    return jnp.sum(jnp.where(spread, column, 0.0), axis=0, keepdims=True)


def scale_cols(sc_ref, start, count, blk):
    rows = sc_ref.shape[0]
    hot = iota((rows, count), 0) == (start + iota((rows, count), 1)) // blk
    return contract0(jnp.exp2(sc_ref[...].astype(F32)).astype(BF16), hot.astype(BF16))


def end_kernel(x_ref, b_ref, st_ref, dl_ref, sc_ref, msg_ref, hs, ds, *, blk):
    step = pl.program_id(0)
    span, chans = x_ref.shape
    heads = st_ref.shape[0]
    states = b_ref.shape[1]

    @pl.when(step == 0)
    def _():
        hs[...] = jnp.zeros_like(hs)
        ds[...] = jnp.ones_like(ds)

    later = (iota((span, span), 0) > iota((span, span), 1)).astype(BF16)
    decay = dl_ref[...]
    tail = summed_over(decay, later)
    w = jnp.exp(tail) * st_ref[...] * scale_cols(sc_ref, step * span, span, blk)
    spread = spread_of(heads, chans)
    hot = spread.astype(BF16)
    wide = contract0(split2(w), jnp.concatenate([hot, hot], axis=0))
    xw = (x_ref[...].astype(F32) * wide).astype(BF16)
    keep = lanes_of(jnp.exp(jnp.sum(decay, axis=1, keepdims=True)), spread)
    hs[...] = keep * hs[...] + contract0(b_ref[...], xw)
    ds[...] = keep * ds[...]

    @pl.when(step == pl.num_programs(0) - 1)
    def _():
        msg_ref[:states, :] = hs[...].astype(BF16)
        total = ds[...]
        high = total.astype(BF16)
        low = (total - high.astype(F32)).astype(BF16)
        msg_ref[states:, :] = jnp.concatenate([high, low], axis=0)


def local_kernel(x_ref, g_ref, b_ref, c_ref, st_ref, dl_ref, sc_ref, sk_ref, a_ref, w_ref, hs, gr, *, blk):
    step = pl.program_id(0)
    span, chans = x_ref.shape
    heads = st_ref.shape[0]

    @pl.when(step == 0)
    def _():
        hs[...] = jnp.zeros_like(hs)
        gr[...] = jnp.ones_like(gr)

    decay = dl_ref[...]
    row = iota((span, span), 0)
    col = iota((span, span), 1)
    same = row // SUB == col // SUB
    upto = jnp.where(row <= col, 1.0, 0.0) - jnp.where(row % SUB < SUB // 2, 1.0, 0.0)
    rel = summed_over(decay, jnp.where(same, upto, 0.0).astype(BF16))
    scale = scale_cols(sc_ref, step * span, span, blk)
    u = jnp.exp(rel)
    v = jnp.exp(-rel) * st_ref[...] * scale
    spread = spread_of(heads, chans)
    hot = spread.astype(BF16)
    hot2 = jnp.concatenate([hot, hot], axis=0)
    u_wide = contract0(split2(u), hot2)
    v_wide = contract0(split2(v), hot2)
    skip = lanes_of(turned(sk_ref[...]) * scale[:, :1], spread)
    x = x_ref[...].astype(F32)
    xv = (x * v_wide).astype(BF16)
    b = b_ref[...]
    c = c_ref[...]
    scores = lax.dot_general(c, b, (((1,), (1,)), ((), ())), preferred_element_type=F32)
    scores = jnp.where(same & (row >= col), scores, 0.0).astype(BF16)
    place = iota((heads, span), 1)
    g = g_ref[...].astype(F32)
    gate = 0.5 * g
    gate = gate + gate * jnp.tanh(gate)
    for part in range(span // SUB):
        lo = part * SUB
        hi = lo + SUB
        first = (place >= lo) & (place < lo + SUB // 2)
        second = (place >= lo + SUB // 2) & (place < hi)
        head_in = lanes_of(jnp.exp(jnp.sum(jnp.where(first, decay, 0.0), axis=1, keepdims=True)), spread)
        head_out = lanes_of(jnp.exp(jnp.sum(jnp.where(second, decay, 0.0), axis=1, keepdims=True)), spread)
        mid = head_in * hs[...]
        lhs = jnp.concatenate([scores[lo:hi], c[lo:hi]], axis=1)
        rhs = jnp.concatenate([xv, mid.astype(BF16)], axis=0)
        acc = jnp.dot(lhs, rhs, preferred_element_type=F32)
        hs[...] = head_out * (mid + contract0(b[lo:hi], xv[lo:hi]))
        mid_growth = head_in * gr[0:1, :]
        gr[...] = jnp.broadcast_to(head_out * mid_growth, gr.shape)
        u_gate = u_wide[lo:hi] * gate[lo:hi]
        a_ref[lo:hi, :] = (u_gate * acc + skip * x[lo:hi] * gate[lo:hi]).astype(BF16)
        w_ref[lo:hi, :] = (u_gate * mid_growth).astype(BF16)


def turned(row):
    return jnp.broadcast_to(row, (8, row.shape[1])).T[:, :1]


def keep_of(ref, lanes=slice(None)):
    rows = ref.shape[0]
    return ref[rows - 16 : rows - 15, lanes].astype(F32) + ref[rows - 8 : rows - 7, lanes].astype(F32)


def chip_kernel(own_ref, other_ref, o_ref):
    core = lax.rem(lax.axis_index("ctx"), 2)
    states = own_ref.shape[0] - 16
    half = o_ref.shape[1]
    lanes = pl.ds(pl.multiple_of(core * half, 128), half)
    own = own_ref[:states, lanes].astype(F32)
    other = other_ref[:states, lanes].astype(F32)
    own_keep = keep_of(own_ref, lanes)
    other_keep = keep_of(other_ref, lanes)
    total = jnp.where(core == 0, other_keep * own + other, own_keep * other + own)
    keep = own_keep * other_keep
    o_ref[:states, :] = total.astype(BF16)
    high = keep.astype(BF16)
    low = (keep - high.astype(F32)).astype(BF16)
    o_ref[states : states + 8, :] = jnp.broadcast_to(high, (8, half))
    o_ref[states + 8 :, :] = jnp.broadcast_to(low, (8, half))


def prior_kernel(*refs):
    o_ref = refs[-1]
    chip = lax.axis_index("ctx") // 2
    states = o_ref.shape[0]
    chips = [jnp.bitwise_xor(chip, k + 1) for k in range(len(refs) - 1)]
    keeps = [keep_of(ref) for ref in refs[:-1]]
    total = jnp.zeros(o_ref.shape, F32)
    for k, ref in enumerate(refs[:-1]):
        weight = jnp.ones_like(keeps[k])
        for other, keep in zip(chips, keeps):
            weight = jnp.where((other > chips[k]) & (other < chip), weight * keep, weight)
        weight = jnp.where(chips[k] < chip, weight, jnp.zeros_like(weight))
        total = total + weight * ref[:states, :].astype(F32)
    o_ref[...] = total.astype(BF16)


def norm_kernel(flip_ref, c_ref, a_ref, w_ref, gain_ref, slot_ref, h_ref, *refs, width):
    n_ref, d_ref, acc, start = refs[-4:]
    step = pl.program_id(0)
    span, half = a_ref.shape

    @pl.when(step == 0)
    def _():
        acc[...] = jnp.zeros_like(acc)
        if len(refs) > 4:
            prior = h_ref[...].astype(F32)
            states = prior.shape[0]
            before = keep_of(refs[0]) * prior + refs[0][:states, :].astype(F32)
            start[...] = jnp.where(flip_ref[0] == 1, before, prior).astype(BF16)
        else:
            start[...] = h_ref[...]

    group = min(256, half)
    same = iota((group, group), 0) // width == iota((group, group), 1) // width
    mean_of = jnp.where(same, 1.0 / width, 0.0).astype(BF16)
    for k in range(0, half, group):
        for r in range(0, span, 128):
            handed = jnp.dot(c_ref[r : r + 128, :], start[:, k : k + group], preferred_element_type=F32)
            t = a_ref[r : r + 128, k : k + group].astype(F32) + w_ref[r : r + 128, k : k + group].astype(F32) * handed
            mean = jnp.dot((t * t).astype(BF16), mean_of, preferred_element_type=F32)
            normed = t * lax.rsqrt(mean + 1e-05) * gain_ref[:, k : k + group]
            n_ref[r : r + 128, k : k + group] = normed.astype(BF16)
    pick = (iota((CAP, span), 0) == slot_ref[...]).astype(BF16)
    acc[...] = acc[...] + jnp.dot(pick, n_ref[...], preferred_element_type=F32)

    @pl.when(step == pl.num_programs(0) - 1)
    def _():
        d_ref[...] = acc[...].astype(BF16)


def expert_kernel(flip_ref, *refs, ring, shards, groups, half):
    halves = len(groups)
    count = sum(map(sum, groups))
    inputs = refs[:count]
    hbm = refs[count : count + 2 * shards]
    outs = refs[count + 2 * shards : count + 2 * shards + ring]
    act, terms = refs[count + 2 * shards + ring :]
    z = lax.axis_index("exp")
    c = lax.axis_index("ctx")
    rows = inputs[0].shape[0]
    chans = half * halves
    at = 0
    for q in range(halves):
        lanes = pl.ds(pl.multiple_of(jnp.bitwise_xor(flip_ref[0], q) * half, 128), half)
        for k in range(ring):
            piece = inputs[at][...]
            for other in range(at + 1, at + groups[q][k]):
                piece = piece + inputs[other][...]
            act[k, :, lanes] = piece
            at += groups[q][k]
    feats = hbm[0].shape[0]
    total = jnp.zeros((rows, hbm[0].shape[1]), F32)
    for k in range(shards):
        first = jnp.bitwise_xor(c, k) * feats
        a = act[jnp.bitwise_xor(z, first // chans), :, pl.ds(pl.multiple_of(lax.rem(first, chans), 128), feats)]
        total = total + jnp.dot(a, hbm[k][...], preferred_element_type=F32)
    hidden = (total / (1.0 + jnp.exp(-total))).astype(BF16)
    cols = hbm[shards].shape[1]
    for k in range(shards):
        first = jnp.bitwise_xor(c, k) * cols
        term = jnp.dot(hidden, hbm[shards + k][...], preferred_element_type=F32).astype(BF16)
        terms[jnp.bitwise_xor(z, first // chans), :, pl.ds(pl.multiple_of(lax.rem(first, chans), 128), cols)] = term
    for k in range(ring):
        outs[k][...] = terms[k]


def final_kernel(flip_ref, slot_ref, prob_ref, *refs, base, count):
    rests = refs[:count]
    terms = refs[count:-2]
    o_ref, sums = refs[-2:]
    rows = sums.shape[0]

    @pl.when(pl.program_id(0) == 0)
    def _():
        total = terms[0][...].astype(F32)
        for other in terms[1:]:
            total = total + other[...].astype(F32)
        sums[...] = total.astype(BF16)

    span = o_ref.shape[0]
    slot = turned(slot_ref[...].astype(F32)).astype(jnp.int32)
    prob = turned(prob_ref[...])
    pick = (iota((span, rows), 1) + base == slot).astype(BF16)
    part = o_ref.shape[1] // count
    for q in range(count):
        lanes = slice(None)
        if count > 1:
            lanes = pl.ds(pl.multiple_of(jnp.bitwise_xor(flip_ref[0], q) * part, 128), part)
        token = jnp.dot(pick, sums[:, lanes], preferred_element_type=F32)
        o_ref[:, lanes] = (rests[q][...].astype(F32) + prob * token).astype(BF16)


def params(size=16):
    return pltpu.CompilerParams(vmem_limit_bytes=size * MIB)


def rows_spec(span, cols):
    return pl.BlockSpec((span, cols), lambda i, *_: (i, 0))


def cols_spec(rows, span):
    return pl.BlockSpec((rows, span), lambda i, *_: (0, i))


def whole(shape):
    return pl.BlockSpec(shape, lambda i, *_: (0,) * len(shape))


def swap(value, axis, count, mask):
    return lax.ppermute(value, axis, [(i, i ^ mask) for i in range(count)])


def gather_pieces(value, axis, count, order):
    pieces = {0: value}
    if count == 8:
        far, near = order
        pieces[far] = swap(value, axis, count, far)
        pieces[near] = swap(value, axis, count, near)
        pieces[6] = swap(pieces[far], axis, count, near)
        for key in (0, far, near, 6):
            pieces[key ^ 1] = swap(pieces[key], axis, count, 1)
    else:
        mask = 1
        while mask < count:
            for key in list(pieces):
                pieces[key ^ mask] = swap(pieces[key], axis, count, mask)
            mask *= 2
    return [pieces[k] for k in range(count)]


ENDS = [(0, 1), (3, 2)]
MIDDLE = [(1, 2), (2, 1)]
OUTWARD = [(1, 0), (2, 3)]


def gather_line(own, ring):
    if ring != 4:
        return [own] + [swap(own, "exp", ring, k) for k in range(1, ring)], [1] * ring
    beside = swap(own, "exp", ring, 1)
    cross = lax.ppermute(own, "exp", MIDDLE)
    cross_far = lax.ppermute(beside, "exp", MIDDLE)
    out_near = lax.ppermute(cross, "exp", OUTWARD)
    out_far = lax.ppermute(cross_far, "exp", OUTWARD)
    return [own, beside, cross_far, out_near, cross, out_far], [1, 1, 2, 2]


def added(a, b):
    return (a.astype(F32) + b.astype(F32)).astype(BF16)


def sum_line(terms, ring):
    if ring != 4:
        return [terms[0]] + [swap(terms[k], "exp", ring, k) for k in range(1, ring)]
    far = lax.ppermute(terms[3], "exp", ENDS)
    near = lax.ppermute(terms[2], "exp", ENDS)
    far = lax.ppermute(added(terms[2], far), "exp", MIDDLE)
    near = lax.ppermute(added(terms[3], near), "exp", MIDDLE)
    beside = swap(added(terms[1], far), "exp", ring, 1)
    return [terms[0], near, beside]


def entering_state(message, states, axis, count):
    def parts(m):
        end = m[:states].astype(F32)
        keep = m[states : states + 1].astype(F32) + m[states + 8 : states + 9].astype(F32)
        return end, keep

    def pack(end, keep):
        high = keep.astype(BF16)
        low = (keep - high.astype(F32)).astype(BF16)
        rows = (8, keep.shape[1])
        return jnp.concatenate([end.astype(BF16), jnp.broadcast_to(high, rows), jnp.broadcast_to(low, rows)], axis=0)

    index = lax.axis_index(axis)
    end, keep = parts(message)
    prior = jnp.zeros_like(end)
    before = jnp.ones_like(keep)
    mask = 1
    while mask < count:
        got_end, got_keep = parts(swap(message, axis, count, mask))
        above = (index & mask) != 0
        prior = jnp.where(above, prior + before * got_end, prior)
        before = jnp.where(above, before * got_keep, before)
        mask *= 2
        if mask < count:
            end = jnp.where(above, keep * got_end + end, got_keep * end + got_end)
            keep = keep * got_keep
            message = pack(end, keep)
    return prior.astype(BF16)


def body(ctx, ring, mixer_input, scale_exponent, step_size, decay_log, state_input, state_output, skip_gain,
         gate_input, norm_gain, up_weight, down_weight, expert_slot, gate_prob):
    tokens, chans = mixer_input.shape
    heads = skip_gain.shape[0]
    states = state_input.shape[1]
    width = chans // heads
    blk = tokens // scale_exponent.shape[0]
    halves = parts = 2
    half = chans // halves
    rows = CAP // parts
    paired = ctx == 8
    flip = lax.rem(lax.axis_index("ctx"), 2)[None] if paired else jnp.zeros((1,), jnp.int32)

    span = 256
    wide = min(512, tokens)
    message = pl.pallas_call(
        functools.partial(end_kernel, blk=blk),
        grid=(tokens // span,),
        in_specs=[rows_spec(span, chans), rows_spec(span, states), cols_spec(heads, span), cols_spec(heads, span),
                  whole(scale_exponent.shape)],
        out_specs=whole((states + 16, chans)),
        out_shape=jax.ShapeDtypeStruct((states + 16, chans), BF16),
        scratch_shapes=[pltpu.VMEM((states, chans), F32), pltpu.VMEM((8, chans), F32)],
        compiler_params=params(60),
        name="end_state",
    )(mixer_input, state_input, step_size, decay_log, scale_exponent)

    if paired:
        beside = swap(message, "ctx", ctx, 1)
        chip_shape = jax.ShapeDtypeStruct((states + 16, half), BF16)
        chip = pl.pallas_call(
            chip_kernel, out_shape=chip_shape, compiler_params=params(), name="chip_state"
        )(message, beside)
        chips = [swap(chip, "ctx", ctx, mask) for mask in (2, 4, 6)]
        prior = pl.pallas_call(
            prior_kernel,
            out_shape=jax.ShapeDtypeStruct((states, half), BF16),
            compiler_params=params(),
            name="prior",
        )(*chips)
        priors = [prior, swap(prior, "ctx", ctx, 1)]
    else:
        start = entering_state(message, states, "ctx", ctx)

    local, weight = pl.pallas_call(
        functools.partial(local_kernel, blk=blk),
        grid=(tokens // blk,),
        in_specs=[rows_spec(blk, chans), rows_spec(blk, chans), rows_spec(blk, states), rows_spec(blk, states),
                  cols_spec(heads, blk), cols_spec(heads, blk), whole(scale_exponent.shape), whole((1, heads))],
        out_specs=[rows_spec(blk, chans), rows_spec(blk, chans)],
        out_shape=[jax.ShapeDtypeStruct((tokens, chans), BF16)] * 2,
        scratch_shapes=[pltpu.VMEM((states, chans), F32), pltpu.VMEM((8, chans), F32)],
        compiler_params=params(48),
        name="local_out",
    )(mixer_input, gate_input, state_input, state_output, step_size, decay_log, scale_exponent,
      skip_gain[None])

    normed = []
    dispatched = []
    for q in range(halves):

        def col(i, flip, q=q):
            return (0, jnp.bitwise_xor(flip[0], q))

        def block(i, flip, q=q):
            return (i, jnp.bitwise_xor(flip[0], q))

        if paired:
            entry = [whole((states, half)), pl.BlockSpec((states + 16, half), col)]
            values = [priors[q], beside]
        else:
            entry = [pl.BlockSpec((states, half), col)]
            values = [start]
        outs = pl.pallas_call(
            functools.partial(norm_kernel, width=width),
            grid_spec=pltpu.PrefetchScalarGridSpec(
                num_scalar_prefetch=1,
                grid=(tokens // wide,),
                in_specs=[rows_spec(wide, states), pl.BlockSpec((wide, half), block), pl.BlockSpec((wide, half), block),
                          pl.BlockSpec((1, half), col), cols_spec(1, wide)] + entry,
                out_specs=[rows_spec(wide, half), whole((CAP, half))],
                scratch_shapes=[pltpu.VMEM((CAP, half), F32), pltpu.VMEM((states, half), BF16)],
            ),
            out_shape=[jax.ShapeDtypeStruct((tokens, half), BF16), jax.ShapeDtypeStruct((CAP, half), BF16)],
            compiler_params=params(),
        )(flip, state_output, local, weight, norm_gain[None], expert_slot[None], *values)
        normed.append(outs[0])
        dispatched.append(outs[1])

    ups = gather_pieces(up_weight, "ctx", ctx, (2, 4))
    downs = gather_pieces(down_weight, "ctx", ctx, (4, 2))

    pieces = []
    groups = []
    for q in range(halves):
        got, group = gather_line(dispatched[q], ring)
        pieces += got
        groups.append(group)

    any_spec = pl.BlockSpec(memory_space=pltpu.VMEM)
    rests = normed
    summed = []
    for part in range(parts):
        terms = pl.pallas_call(
            functools.partial(expert_kernel, ring=ring, shards=ctx, groups=groups, half=half),
            grid_spec=pltpu.PrefetchScalarGridSpec(
                num_scalar_prefetch=1,
                grid=(1,),
                in_specs=[pl.BlockSpec((rows, half), lambda i, flip, part=part: (part, 0))] * len(pieces)
                + [any_spec] * (2 * ctx),
                out_specs=[whole((rows, chans))] * ring,
                scratch_shapes=[
                    pltpu.VMEM((ring, rows, chans), BF16),
                    pltpu.VMEM((ring, rows, chans), BF16),
                ],
            ),
            out_shape=[jax.ShapeDtypeStruct((rows, chans), BF16)] * ring,
            compiler_params=params(26),
        )(flip, *pieces, *ups, *downs)
        summed.append(sum_line(terms, ring))

    for part in range(parts):
        rests = [pl.pallas_call(
            functools.partial(final_kernel, base=part * rows, count=len(rests)),
            grid_spec=pltpu.PrefetchScalarGridSpec(
                num_scalar_prefetch=1,
                grid=(tokens // wide,),
                in_specs=[cols_spec(1, wide), cols_spec(1, wide)]
                + [rows_spec(wide, chans // len(rests))] * len(rests)
                + [whole((rows, chans))] * len(summed[part]),
                out_specs=rows_spec(wide, chans),
                scratch_shapes=[pltpu.VMEM((rows, chans), BF16)],
            ),
            out_shape=jax.ShapeDtypeStruct((tokens, chans), BF16),
            compiler_params=params(),
        )(flip, expert_slot[None], gate_prob[None], *rests, *summed[part])]
    return rests[0]


def solution(mesh):
    in_specs = (
        P("ctx", "exp"),
        P("ctx", "exp"),
        P("exp", "ctx"),
        P("exp", "ctx"),
        P("ctx", None),
        P("ctx", None),
        P("exp"),
        P("ctx", "exp"),
        P("exp"),
        P("ctx", "exp"),
        P("exp", "ctx"),
        P("ctx"),
        P("ctx"),
    )
    ctx, ring = mesh.shape["ctx"], mesh.shape["exp"]

    def run(*arrays):
        return body(ctx, ring, *arrays)

    return jax.shard_map(run, mesh=mesh, in_specs=in_specs, out_specs=P("ctx", "exp"), check_vma=False)
```

```python
import functools

import jax
import jax.numpy as jnp
from jax import lax
from jax.experimental import pallas as pl
from jax.experimental.pallas import tpu as pltpu
from jax.sharding import PartitionSpec as P


CAP = 256
SUB = 64
F32 = jnp.float32
BF16 = jnp.bfloat16
MIB = 1024 * 1024


def iota(shape, dim):
    return lax.broadcasted_iota(jnp.int32, shape, dim)


def contract0(a, b):
    return lax.dot_general(a, b, (((0,), (0,)), ((), ())), preferred_element_type=F32)


def split2(v):
    high = v.astype(BF16)
    return jnp.concatenate([high, (v - high.astype(F32)).astype(BF16)], axis=0)


def summed_over(decay, pattern):
    heads = decay.shape[0]
    high = decay.astype(BF16)
    rest = decay - high.astype(F32)
    middle = rest.astype(BF16)
    low = (rest - middle.astype(F32)).astype(BF16)
    total = jnp.dot(jnp.concatenate([high, middle, low], axis=0), pattern, preferred_element_type=F32)
    return total[:heads] + total[heads : 2 * heads] + total[2 * heads :]


def spread_of(heads, chans):
    return iota((heads, chans), 1) // (chans // heads) == iota((heads, chans), 0)


def lanes_of(column, spread):
    return jnp.sum(jnp.where(spread, column, 0.0), axis=0, keepdims=True)


def scale_cols(sc_ref, start, count, blk):
    rows = sc_ref.shape[0]
    hot = iota((rows, count), 0) == (start + iota((rows, count), 1)) // blk
    return contract0(jnp.exp2(sc_ref[...].astype(F32)).astype(BF16), hot.astype(BF16))


def end_kernel(x_ref, b_ref, st_ref, dl_ref, sc_ref, msg_ref, hs, ds, *, blk):
    step = pl.program_id(0)
    span, chans = x_ref.shape
    heads = st_ref.shape[0]
    states = b_ref.shape[1]

    @pl.when(step == 0)
    def _():
        hs[...] = jnp.zeros_like(hs)
        ds[...] = jnp.ones_like(ds)

    later = (iota((span, span), 0) > iota((span, span), 1)).astype(BF16)
    decay = dl_ref[...]
    tail = summed_over(decay, later)
    w = jnp.exp(tail) * st_ref[...] * scale_cols(sc_ref, step * span, span, blk)
    spread = spread_of(heads, chans)
    hot = spread.astype(BF16)
    wide = contract0(split2(w), jnp.concatenate([hot, hot], axis=0))
    xw = (x_ref[...].astype(F32) * wide).astype(BF16)
    keep = lanes_of(jnp.exp(jnp.sum(decay, axis=1, keepdims=True)), spread)
    hs[...] = keep * hs[...] + contract0(b_ref[...], xw)
    ds[...] = keep * ds[...]

    @pl.when(step == pl.num_programs(0) - 1)
    def _():
        msg_ref[:states, :] = hs[...].astype(BF16)
        total = ds[...]
        high = total.astype(BF16)
        low = (total - high.astype(F32)).astype(BF16)
        msg_ref[states:, :] = jnp.concatenate([high, low], axis=0)


def local_kernel(x_ref, g_ref, b_ref, c_ref, st_ref, dl_ref, sc_ref, sk_ref, a_ref, w_ref, hs, gr, *, blk):
    step = pl.program_id(0)
    span, chans = x_ref.shape
    heads = st_ref.shape[0]

    @pl.when(step == 0)
    def _():
        hs[...] = jnp.zeros_like(hs)
        gr[...] = jnp.ones_like(gr)

    decay = dl_ref[...]
    row = iota((span, span), 0)
    col = iota((span, span), 1)
    same = row // SUB == col // SUB
    upto = jnp.where(row <= col, 1.0, 0.0) - jnp.where(row % SUB < SUB // 2, 1.0, 0.0)
    rel = summed_over(decay, jnp.where(same, upto, 0.0).astype(BF16))
    scale = scale_cols(sc_ref, step * span, span, blk)
    u = jnp.exp(rel)
    v = jnp.exp(-rel) * st_ref[...] * scale
    spread = spread_of(heads, chans)
    hot = spread.astype(BF16)
    hot2 = jnp.concatenate([hot, hot], axis=0)
    u_wide = contract0(split2(u), hot2)
    v_wide = contract0(split2(v), hot2)
    skip = lanes_of(turned(sk_ref[...]) * scale[:, :1], spread)
    x = x_ref[...].astype(F32)
    xv = (x * v_wide).astype(BF16)
    b = b_ref[...]
    c = c_ref[...]
    scores = lax.dot_general(c, b, (((1,), (1,)), ((), ())), preferred_element_type=F32)
    scores = jnp.where(same & (row >= col), scores, 0.0).astype(BF16)
    place = iota((heads, span), 1)
    g = g_ref[...].astype(F32)
    gate = 0.5 * g
    gate = gate + gate * jnp.tanh(gate)
    for part in range(span // SUB):
        lo = part * SUB
        hi = lo + SUB
        first = (place >= lo) & (place < lo + SUB // 2)
        second = (place >= lo + SUB // 2) & (place < hi)
        head_in = lanes_of(jnp.exp(jnp.sum(jnp.where(first, decay, 0.0), axis=1, keepdims=True)), spread)
        head_out = lanes_of(jnp.exp(jnp.sum(jnp.where(second, decay, 0.0), axis=1, keepdims=True)), spread)
        mid = head_in * hs[...]
        lhs = jnp.concatenate([scores[lo:hi], c[lo:hi]], axis=1)
        rhs = jnp.concatenate([xv, mid.astype(BF16)], axis=0)
        acc = jnp.dot(lhs, rhs, preferred_element_type=F32)
        hs[...] = head_out * (mid + contract0(b[lo:hi], xv[lo:hi]))
        mid_growth = head_in * gr[0:1, :]
        gr[...] = jnp.broadcast_to(head_out * mid_growth, gr.shape)
        u_gate = u_wide[lo:hi] * gate[lo:hi]
        a_ref[lo:hi, :] = (u_gate * acc + skip * x[lo:hi] * gate[lo:hi]).astype(BF16)
        w_ref[lo:hi, :] = (u_gate * mid_growth).astype(BF16)


def turned(row):
    return jnp.broadcast_to(row, (8, row.shape[1])).T[:, :1]


def keep_of(ref, lanes=slice(None)):
    rows = ref.shape[0]
    return ref[rows - 16 : rows - 15, lanes].astype(F32) + ref[rows - 8 : rows - 7, lanes].astype(F32)


def chip_kernel(own_ref, other_ref, o_ref):
    core = lax.rem(lax.axis_index("ctx"), 2)
    states = own_ref.shape[0] - 16
    half = o_ref.shape[1]
    lanes = pl.ds(pl.multiple_of(core * half, 128), half)
    own = own_ref[:states, lanes].astype(F32)
    other = other_ref[:states, lanes].astype(F32)
    own_keep = keep_of(own_ref, lanes)
    other_keep = keep_of(other_ref, lanes)
    total = jnp.where(core == 0, other_keep * own + other, own_keep * other + own)
    keep = own_keep * other_keep
    o_ref[:states, :] = total.astype(BF16)
    high = keep.astype(BF16)
    low = (keep - high.astype(F32)).astype(BF16)
    o_ref[states : states + 8, :] = jnp.broadcast_to(high, (8, half))
    o_ref[states + 8 :, :] = jnp.broadcast_to(low, (8, half))


def prior_kernel(*refs):
    o_ref = refs[-1]
    chip = lax.axis_index("ctx") // 2
    states = o_ref.shape[0]
    chips = [jnp.bitwise_xor(chip, k + 1) for k in range(len(refs) - 1)]
    keeps = [keep_of(ref) for ref in refs[:-1]]
    total = jnp.zeros(o_ref.shape, F32)
    for k, ref in enumerate(refs[:-1]):
        weight = jnp.ones_like(keeps[k])
        for other, keep in zip(chips, keeps):
            weight = jnp.where((other > chips[k]) & (other < chip), weight * keep, weight)
        weight = jnp.where(chips[k] < chip, weight, jnp.zeros_like(weight))
        total = total + weight * ref[:states, :].astype(F32)
    o_ref[...] = total.astype(BF16)


def norm_kernel(flip_ref, c_ref, a_ref, w_ref, gain_ref, slot_ref, h_ref, *refs, width):
    n_ref, d_ref, acc, start = refs[-4:]
    step = pl.program_id(0)
    span, half = a_ref.shape

    @pl.when(step == 0)
    def _():
        acc[...] = jnp.zeros_like(acc)
        if len(refs) > 4:
            prior = h_ref[...].astype(F32)
            states = prior.shape[0]
            before = keep_of(refs[0]) * prior + refs[0][:states, :].astype(F32)
            start[...] = jnp.where(flip_ref[0] == 1, before, prior).astype(BF16)
        else:
            start[...] = h_ref[...]

    group = min(256, half)
    same = iota((group, group), 0) // width == iota((group, group), 1) // width
    mean_of = jnp.where(same, 1.0 / width, 0.0).astype(BF16)
    for k in range(0, half, group):
        for r in range(0, span, 128):
            handed = jnp.dot(c_ref[r : r + 128, :], start[:, k : k + group], preferred_element_type=F32)
            t = a_ref[r : r + 128, k : k + group].astype(F32) + w_ref[r : r + 128, k : k + group].astype(F32) * handed
            mean = jnp.dot((t * t).astype(BF16), mean_of, preferred_element_type=F32)
            normed = t * lax.rsqrt(mean + 1e-05) * gain_ref[:, k : k + group]
            n_ref[r : r + 128, k : k + group] = normed.astype(BF16)
    pick = (iota((CAP, span), 0) == slot_ref[...]).astype(BF16)
    acc[...] = acc[...] + jnp.dot(pick, n_ref[...], preferred_element_type=F32)

    @pl.when(step == pl.num_programs(0) - 1)
    def _():
        d_ref[...] = acc[...].astype(BF16)


def expert_kernel(flip_ref, *refs, ring, shards, groups, half):
    halves = len(groups)
    count = sum(map(sum, groups))
    inputs = refs[:count]
    hbm = refs[count : count + 2 * shards]
    outs = refs[count + 2 * shards : count + 2 * shards + ring]
    act, terms = refs[count + 2 * shards + ring :]
    z = lax.axis_index("exp")
    c = lax.axis_index("ctx")
    rows = inputs[0].shape[0]
    chans = half * halves
    at = 0
    for q in range(halves):
        lanes = pl.ds(pl.multiple_of(jnp.bitwise_xor(flip_ref[0], q) * half, 128), half)
        for k in range(ring):
            piece = inputs[at][...]
            for other in range(at + 1, at + groups[q][k]):
                piece = piece + inputs[other][...]
            act[k, :, lanes] = piece
            at += groups[q][k]
    feats = hbm[0].shape[0]
    total = jnp.zeros((rows, hbm[0].shape[1]), F32)
    for k in range(shards):
        first = jnp.bitwise_xor(c, k) * feats
        a = act[jnp.bitwise_xor(z, first // chans), :, pl.ds(pl.multiple_of(lax.rem(first, chans), 128), feats)]
        total = total + jnp.dot(a, hbm[k][...], preferred_element_type=F32)
    hidden = (total / (1.0 + jnp.exp(-total))).astype(BF16)
    cols = hbm[shards].shape[1]
    for k in range(shards):
        first = jnp.bitwise_xor(c, k) * cols
        term = jnp.dot(hidden, hbm[shards + k][...], preferred_element_type=F32).astype(BF16)
        terms[jnp.bitwise_xor(z, first // chans), :, pl.ds(pl.multiple_of(lax.rem(first, chans), 128), cols)] = term
    for k in range(ring):
        outs[k][...] = terms[k]


def final_kernel(flip_ref, slot_ref, prob_ref, *refs, base, count):
    rests = refs[:count]
    terms = refs[count:-2]
    o_ref, sums = refs[-2:]
    rows = sums.shape[0]

    @pl.when(pl.program_id(0) == 0)
    def _():
        total = terms[0][...].astype(F32)
        for other in terms[1:]:
            total = total + other[...].astype(F32)
        sums[...] = total.astype(BF16)

    span = o_ref.shape[0]
    slot = turned(slot_ref[...].astype(F32)).astype(jnp.int32)
    prob = turned(prob_ref[...])
    pick = (iota((span, rows), 1) + base == slot).astype(BF16)
    part = o_ref.shape[1] // count
    for q in range(count):
        lanes = slice(None)
        if count > 1:
            lanes = pl.ds(pl.multiple_of(jnp.bitwise_xor(flip_ref[0], q) * part, 128), part)
        token = jnp.dot(pick, sums[:, lanes], preferred_element_type=F32)
        o_ref[:, lanes] = (rests[q][...].astype(F32) + prob * token).astype(BF16)


def last_kernel(slot_ref, prob_ref, rest_ref, *refs, base, span):
    terms = refs[:-3]
    o_hbm, out, sem = refs[-3:]
    total = terms[0][...].astype(F32)
    for other in terms[1:]:
        total = total + other[...].astype(F32)
    sums = total.astype(BF16)
    rows = sums.shape[0]
    copies = []
    for k in range(out.shape[0] // span):
        lines = slice(k * span, (k + 1) * span)
        slot = turned(slot_ref[:, lines].astype(F32)).astype(jnp.int32)
        pick = (iota((span, rows), 1) + base == slot).astype(BF16)
        token = jnp.dot(pick, sums, preferred_element_type=F32)
        out[lines, :] = (rest_ref[lines, :].astype(F32) + turned(prob_ref[:, lines]) * token).astype(BF16)
        copies.append(pltpu.make_async_copy(out.at[pl.ds(k * span, span)], o_hbm.at[pl.ds(k * span, span)], sem.at[k]))
        copies[k].start()
    for copy in copies:
        copy.wait()


def params(size=16):
    return pltpu.CompilerParams(vmem_limit_bytes=size * MIB)


def rows_spec(span, cols):
    return pl.BlockSpec((span, cols), lambda i, *_: (i, 0))


def cols_spec(rows, span):
    return pl.BlockSpec((rows, span), lambda i, *_: (0, i))


def whole(shape):
    return pl.BlockSpec(shape, lambda i, *_: (0,) * len(shape))


def swap(value, axis, count, mask):
    return lax.ppermute(value, axis, [(i, i ^ mask) for i in range(count)])


def gather_pieces(value, axis, count, order):
    pieces = {0: value}
    if count == 8:
        far, near = order
        pieces[far] = swap(value, axis, count, far)
        pieces[near] = swap(value, axis, count, near)
        pieces[6] = swap(pieces[far], axis, count, near)
        for key in (0, far, near, 6):
            pieces[key ^ 1] = swap(pieces[key], axis, count, 1)
    else:
        mask = 1
        while mask < count:
            for key in list(pieces):
                pieces[key ^ mask] = swap(pieces[key], axis, count, mask)
            mask *= 2
    return [pieces[k] for k in range(count)]


ENDS = [(0, 1), (3, 2)]
MIDDLE = [(1, 2), (2, 1)]
OUTWARD = [(1, 0), (2, 3)]


def gather_line(own, ring):
    if ring != 4:
        return [own] + [swap(own, "exp", ring, k) for k in range(1, ring)], [1] * ring
    beside = swap(own, "exp", ring, 1)
    cross = lax.ppermute(own, "exp", MIDDLE)
    cross_far = lax.ppermute(beside, "exp", MIDDLE)
    out_near = lax.ppermute(cross, "exp", OUTWARD)
    out_far = lax.ppermute(cross_far, "exp", OUTWARD)
    return [own, beside, cross_far, out_near, cross, out_far], [1, 1, 2, 2]


def added(a, b):
    return (a.astype(F32) + b.astype(F32)).astype(BF16)


def sum_line(terms, ring):
    if ring != 4:
        return [terms[0]] + [swap(terms[k], "exp", ring, k) for k in range(1, ring)]
    far = lax.ppermute(terms[3], "exp", ENDS)
    near = lax.ppermute(terms[2], "exp", ENDS)
    far = lax.ppermute(added(terms[2], far), "exp", MIDDLE)
    near = lax.ppermute(added(terms[3], near), "exp", MIDDLE)
    beside = swap(added(terms[1], far), "exp", ring, 1)
    return [terms[0], near, beside]


def entering_state(message, states, axis, count):
    def parts(m):
        end = m[:states].astype(F32)
        keep = m[states : states + 1].astype(F32) + m[states + 8 : states + 9].astype(F32)
        return end, keep

    def pack(end, keep):
        high = keep.astype(BF16)
        low = (keep - high.astype(F32)).astype(BF16)
        rows = (8, keep.shape[1])
        return jnp.concatenate([end.astype(BF16), jnp.broadcast_to(high, rows), jnp.broadcast_to(low, rows)], axis=0)

    index = lax.axis_index(axis)
    end, keep = parts(message)
    prior = jnp.zeros_like(end)
    before = jnp.ones_like(keep)
    mask = 1
    while mask < count:
        got_end, got_keep = parts(swap(message, axis, count, mask))
        above = (index & mask) != 0
        prior = jnp.where(above, prior + before * got_end, prior)
        before = jnp.where(above, before * got_keep, before)
        mask *= 2
        if mask < count:
            end = jnp.where(above, keep * got_end + end, got_keep * end + got_end)
            keep = keep * got_keep
            message = pack(end, keep)
    return prior.astype(BF16)


def body(ctx, ring, mixer_input, scale_exponent, step_size, decay_log, state_input, state_output, skip_gain,
         gate_input, norm_gain, up_weight, down_weight, expert_slot, gate_prob):
    tokens, chans = mixer_input.shape
    heads = skip_gain.shape[0]
    states = state_input.shape[1]
    width = chans // heads
    blk = tokens // scale_exponent.shape[0]
    halves = parts = 2
    half = chans // halves
    rows = CAP // parts
    paired = ctx == 8
    flip = lax.rem(lax.axis_index("ctx"), 2)[None] if paired else jnp.zeros((1,), jnp.int32)

    span = 256
    wide = min(512, tokens)
    message = pl.pallas_call(
        functools.partial(end_kernel, blk=blk),
        grid=(tokens // span,),
        in_specs=[rows_spec(span, chans), rows_spec(span, states), cols_spec(heads, span), cols_spec(heads, span),
                  whole(scale_exponent.shape)],
        out_specs=whole((states + 16, chans)),
        out_shape=jax.ShapeDtypeStruct((states + 16, chans), BF16),
        scratch_shapes=[pltpu.VMEM((states, chans), F32), pltpu.VMEM((8, chans), F32)],
        compiler_params=params(60),
        name="end_state",
    )(mixer_input, state_input, step_size, decay_log, scale_exponent)

    if paired:
        beside = swap(message, "ctx", ctx, 1)
        chip_shape = jax.ShapeDtypeStruct((states + 16, half), BF16)
        chip = pl.pallas_call(
            chip_kernel, out_shape=chip_shape, compiler_params=params(), name="chip_state"
        )(message, beside)
        chips = [swap(chip, "ctx", ctx, mask) for mask in (2, 4, 6)]
        prior = pl.pallas_call(
            prior_kernel,
            out_shape=jax.ShapeDtypeStruct((states, half), BF16),
            compiler_params=params(),
            name="prior",
        )(*chips)
        priors = [prior, swap(prior, "ctx", ctx, 1)]
    else:
        start = entering_state(message, states, "ctx", ctx)

    local, weight = pl.pallas_call(
        functools.partial(local_kernel, blk=blk),
        grid=(tokens // blk,),
        in_specs=[rows_spec(blk, chans), rows_spec(blk, chans), rows_spec(blk, states), rows_spec(blk, states),
                  cols_spec(heads, blk), cols_spec(heads, blk), whole(scale_exponent.shape), whole((1, heads))],
        out_specs=[rows_spec(blk, chans), rows_spec(blk, chans)],
        out_shape=[jax.ShapeDtypeStruct((tokens, chans), BF16)] * 2,
        scratch_shapes=[pltpu.VMEM((states, chans), F32), pltpu.VMEM((8, chans), F32)],
        compiler_params=params(48),
        name="local_out",
    )(mixer_input, gate_input, state_input, state_output, step_size, decay_log, scale_exponent,
      skip_gain[None])

    normed = []
    dispatched = []
    for q in range(halves):

        def col(i, flip, q=q):
            return (0, jnp.bitwise_xor(flip[0], q))

        def block(i, flip, q=q):
            return (i, jnp.bitwise_xor(flip[0], q))

        if paired:
            entry = [whole((states, half)), pl.BlockSpec((states + 16, half), col)]
            values = [priors[q], beside]
        else:
            entry = [pl.BlockSpec((states, half), col)]
            values = [start]
        outs = pl.pallas_call(
            functools.partial(norm_kernel, width=width),
            grid_spec=pltpu.PrefetchScalarGridSpec(
                num_scalar_prefetch=1,
                grid=(tokens // tokens,),
                in_specs=[rows_spec(tokens, states), pl.BlockSpec((tokens, half), block), pl.BlockSpec((tokens, half), block),
                          pl.BlockSpec((1, half), col), cols_spec(1, tokens)] + entry,
                out_specs=[rows_spec(tokens, half), whole((CAP, half))],
                scratch_shapes=[pltpu.VMEM((CAP, half), F32), pltpu.VMEM((states, half), BF16)],
            ),
            out_shape=[jax.ShapeDtypeStruct((tokens, half), BF16), jax.ShapeDtypeStruct((CAP, half), BF16)],
            compiler_params=params(24),
        )(flip, state_output, local, weight, norm_gain[None], expert_slot[None], *values)
        normed.append(outs[0])
        dispatched.append(outs[1])

    ups = gather_pieces(up_weight, "ctx", ctx, (2, 4))
    downs = gather_pieces(down_weight, "ctx", ctx, (4, 2))

    pieces = []
    groups = []
    for q in range(halves):
        got, group = gather_line(dispatched[q], ring)
        pieces += got
        groups.append(group)

    any_spec = pl.BlockSpec(memory_space=pltpu.VMEM)
    rests = normed
    summed = []
    for part in range(parts):
        terms = pl.pallas_call(
            functools.partial(expert_kernel, ring=ring, shards=ctx, groups=groups, half=half),
            grid_spec=pltpu.PrefetchScalarGridSpec(
                num_scalar_prefetch=1,
                grid=(1,),
                in_specs=[pl.BlockSpec((rows, half), lambda i, flip, part=part: (part, 0))] * len(pieces)
                + [any_spec] * (2 * ctx),
                out_specs=[whole((rows, chans))] * ring,
                scratch_shapes=[
                    pltpu.VMEM((ring, rows, chans), BF16),
                    pltpu.VMEM((ring, rows, chans), BF16),
                ],
            ),
            out_shape=[jax.ShapeDtypeStruct((rows, chans), BF16)] * ring,
            compiler_params=params(10),
        )(flip, *pieces, *ups, *downs)
        summed.append(sum_line(terms, ring))

    for part in range(parts - 1):
        rests = [pl.pallas_call(
            functools.partial(final_kernel, base=part * rows, count=len(rests)),
            grid_spec=pltpu.PrefetchScalarGridSpec(
                num_scalar_prefetch=1,
                grid=(tokens // wide,),
                in_specs=[cols_spec(1, wide), cols_spec(1, wide)]
                + [rows_spec(wide, chans // len(rests))] * len(rests)
                + [whole((rows, chans))] * len(summed[part]),
                out_specs=rows_spec(wide, chans),
                scratch_shapes=[pltpu.VMEM((rows, chans), BF16)],
            ),
            out_shape=jax.ShapeDtypeStruct((tokens, chans), BF16),
            compiler_params=params(),
        )(flip, expert_slot[None], gate_prob[None], *rests, *summed[part])]
    chip = pl.BlockSpec(memory_space=pltpu.VMEM)
    return pl.pallas_call(
        functools.partial(last_kernel, base=(parts - 1) * rows, span=span),
        in_specs=[chip] * (3 + len(summed[-1])),
        out_specs=pl.BlockSpec(memory_space=pl.ANY),
        scratch_shapes=[pltpu.VMEM((tokens, chans), BF16), pltpu.SemaphoreType.DMA((tokens // span,))],
        out_shape=jax.ShapeDtypeStruct((tokens, chans), BF16),
        compiler_params=params(),
        name="combineB",
    )(expert_slot[None], gate_prob[None], *rests, *summed[-1])


def solution(mesh):
    in_specs = (
        P("ctx", "exp"),
        P("ctx", "exp"),
        P("exp", "ctx"),
        P("exp", "ctx"),
        P("ctx", None),
        P("ctx", None),
        P("exp"),
        P("ctx", "exp"),
        P("exp"),
        P("ctx", "exp"),
        P("exp", "ctx"),
        P("ctx"),
        P("ctx"),
    )
    ctx, ring = mesh.shape["ctx"], mesh.shape["exp"]

    def run(*arrays):
        return body(ctx, ring, *arrays)

    return jax.shard_map(run, mesh=mesh, in_specs=in_specs, out_specs=P("ctx", "exp"), check_vma=False)
```
